32 devices in a mesh: region: 4 (over z), enc: 8 (over y, x, core).
Axes of the slice: x: 2, y: 2, z: 4, core: 2. Of those that a mesh axis runs over, the one named last changes fastest.
Arguments:
- pixels: bfloat16 [256, 48, 4096], P(('region', 'enc')), may hold values from -6 to 6
- feature_grad: bfloat16 [256, 96, 4096], P(('region', 'enc')), may hold values from -0.0046691895 to 0.0046691895
- tissue_count: int32 [32], P(('region', 'enc')), may hold values from 1 to 8, as said below
- stem_weight: bfloat16 [96, 48], replicated, may hold values from -0.875 to 0.875
- stem_gain: float32 [96], replicated, may hold values from 0.5 to 1.5
- stem_shift: float32 [96], replicated, may hold values from -3 to 3
- depth_kernel: float32 [96, 49], replicated, may hold values from -0.875 to 0.875
- block_gain: float32 [96], replicated, may hold values from 0.5 to 1.5
- expand_weight: bfloat16 [384, 96], replicated, may hold values from -0.625 to 0.625
- expand_bias: float32 [384], replicated, may hold values from -3 to 3
- reduce_weight: bfloat16 [96, 384], replicated, may hold values from -0.3125 to 0.3125
- layer_scale: float32 [96], replicated, may hold values from 0.5 to 1.5
Outputs:
- features: bfloat16 [256, 96, 4096], P(('region', 'enc'))
- grad_stem: float32 [96, 48], replicated
- grad_gain: float32 [96], replicated
- grad_shift: float32 [96], replicated
- grad_kernel: float32 [96, 49], replicated
- grad_norm: float32 [96], replicated
- grad_expand: float32 [384, 96], replicated
- grad_bias: float32 [384], replicated
- grad_reduce: float32 [96, 384], replicated
- grad_scale: float32 [96], replicated
The draws below stay inside these ranges and needn't reach their ends.
Inputs may be any that keep to these rules, and one draw needn't show every extreme that they name: `tissue_count`: the tissue tiles of a device fill its first slots; the other slots are unused.
All inputs are finite; a program needn't handle non-finite values.
Results may differ from the reference program's by a relative error of at most 0.015.
Values may be sent and summed in bfloat16 or wider, within the bound.
A program may use at most 256 MiB of HBM per device.

```python
from functools import partial
import jax
import jax.numpy as jnp
from jax import lax

C = 96
HID = 384
PATCH = 48
SIDE = 64
KSIZE = 7
SLOTS = 8
TILES = 256
N_REGION = 4
N_ENC = 8


def draw_tissue_count(key, part):
    first, second, fourth = jax.random.split(key, 3)
    shape = (N_REGION * N_ENC,)
    lowest = jnp.minimum(jax.random.randint(first, shape, 1, SLOTS + 1), jax.random.randint(second, shape, 1, SLOTS + 1))
    picked = jax.random.randint(fourth, (N_REGION,), 0, N_ENC)
    device_index = jnp.arange(N_REGION * N_ENC, dtype=jnp.int32)
    filled = device_index % N_ENC == picked[device_index // N_ENC]
    return jnp.where(filled, SLOTS, lowest).astype(jnp.int32)


def steps_of(rng, dims, shards, smallest, largest):
    def one(axis_at, shards_of):
        steps = jax.random.uniform(jax.random.fold_in(jax.random.fold_in(rng, 6), axis_at), (shards_of,), jnp.float32, smallest / len(shards), largest / len(shards))
        return jnp.repeat(jnp.exp(steps), dims[axis_at] // shards_of).reshape((-1,) + (1,) * (len(dims) - axis_at - 1))

    factor_of = one(*shards[0])
    for cut in shards[1:]:
        factor_of = factor_of * one(*cut)
    return factor_of


def gaussian(key, dims, scale, bound, pieces=(), kind=jnp.bfloat16):
    gain = steps_of(key, dims, pieces, -0.22, 0.18) if pieces else 1.0
    values = jax.random.normal(key, dims, jnp.float32) * scale * gain
    return jnp.minimum(jnp.maximum(values, -bound), bound).astype(kind)


def setup_inputs(seed: int = 0) -> dict:
    arg_keys = jax.random.split(jax.random.key(seed), 13)
    return {
        "pixels": gaussian(arg_keys[0], (TILES, PATCH, SIDE * SIDE), 1.0, 6.0, ((0, 32),)),
        "feature_grad": gaussian(arg_keys[1], (TILES, C, SIDE * SIDE), (0.05 / SIDE), 0.0046691895, ((0, 32),)),
        "tissue_count": draw_tissue_count(jax.random.fold_in(arg_keys[12], 71), 0),
        "stem_weight": gaussian(arg_keys[3], (C, PATCH), PATCH ** -0.5, 0.875),
        "stem_gain": jnp.clip(1.0 + 0.1 * jax.random.normal(arg_keys[4], (C,), jnp.float32), 0.5, 1.5),
        "stem_shift": gaussian(arg_keys[5], (C,), 0.5, 3.0, (), jnp.float32),
        "depth_kernel": gaussian(arg_keys[6], (C, KSIZE * KSIZE), (KSIZE * KSIZE) ** -0.5, 0.875, (), jnp.float32),
        "block_gain": jnp.clip(1.0 + 0.1 * jax.random.normal(arg_keys[7], (C,), jnp.float32), 0.5, 1.5),
        "expand_weight": gaussian(arg_keys[8], (HID, C), C ** -0.5, 0.625),
        "expand_bias": gaussian(arg_keys[9], (HID,), 0.5, 3.0, (), jnp.float32),
        "reduce_weight": gaussian(arg_keys[10], (C, HID), HID ** -0.5, 0.3125),
        "layer_scale": jnp.clip(jax.random.uniform(arg_keys[11], (C,), jnp.float32, 0.5, 1.5), 0.5, 1.5),
    }


EPS = 1e-06

def channel_norm(values, channel_gain, channel_shift):
    centre = lax.optimization_barrier(jnp.mean(values, axis=0, keepdims=True))
    spread = lax.optimization_barrier(jnp.mean(jnp.square(values - centre), axis=0, keepdims=True))
    return (values - centre) * lax.rsqrt(spread + EPS) * channel_gain[:, None] + channel_shift[:, None]

def depthwise(values, kernel):
    margin = 3 * SIDE + 3
    padded = jnp.pad(values, ((0, 0), (margin, margin)))
    column = jnp.arange(SIDE * SIDE, dtype=jnp.int32) % SIDE
    result = jnp.zeros_like(values)
    for row_step in range(-3, 4):
        for col_step in range(-3, 4):
            offset = margin + row_step * SIDE + col_step
            shifted = padded[:, offset:offset + SIDE * SIDE]
            inside = (column + col_step >= 0) & (column + col_step < SIDE)
            weight = kernel[:, (row_step + 3) * KSIZE + col_step + 3]
            result = result + weight[:, None] * jnp.where(inside[None, :], shifted, jnp.zeros_like(shifted))
    return result

def forward(weights, tile_pixels):
    stem_weight, stem_gain, stem_shift, depth_kernel, block_gain, expand_weight, expand_bias, reduce_weight, layer_scale = weights
    stem_out = jnp.dot(stem_weight.astype(jnp.bfloat16), tile_pixels, preferred_element_type=jnp.float32)
    base = lax.optimization_barrier(channel_norm(stem_out, stem_gain, stem_shift).astype(jnp.bfloat16))
    mixed = depthwise(base.astype(jnp.float32), depth_kernel)
    normed = channel_norm(mixed, block_gain, jnp.zeros_like(block_gain)).astype(jnp.bfloat16)
    expand = jnp.dot(expand_weight.astype(jnp.bfloat16), normed, preferred_element_type=jnp.float32) + expand_bias[:, None]
    hidden = jax.nn.gelu(expand, approximate=False).astype(jnp.bfloat16)
    reduced = jnp.dot(reduce_weight.astype(jnp.bfloat16), hidden, preferred_element_type=jnp.float32)
    return (base.astype(jnp.float32) + layer_scale[:, None] * reduced).astype(jnp.bfloat16)

def encode(weights, tile_pixels, tile_grad):
    block_out, pullback = jax.vjp(partial(forward, tile_pixels=tile_pixels), weights)
    return (block_out, pullback(tile_grad)[0])

def reference(pixels, feature_grad, tissue_count, stem_weight, stem_gain, stem_shift, depth_kernel, block_gain, expand_weight, expand_bias, reduce_weight, layer_scale):
    weights = tuple((member.astype(jnp.float32) for member in (stem_weight, stem_gain, stem_shift, depth_kernel, block_gain, expand_weight, expand_bias, reduce_weight, layer_scale)))
    slot_index = jnp.arange(pixels.shape[0], dtype=jnp.int32)
    live = slot_index % SLOTS < tissue_count[slot_index // SLOTS]
    zero_grads = jax.tree.map(jnp.zeros_like, weights)

    def scan_step(totals, inputs):
        tile_pixels, tile_grad, occupied = inputs

        def compute(operand):
            return encode(weights, tile_pixels, tile_grad)

        def skipped(operand):
            return (jnp.zeros(tile_grad.shape, tile_grad.dtype), zero_grads)
        block_out, grads = lax.cond(occupied, compute, skipped, 0)
        return (jax.tree.map(jnp.add, totals, grads), block_out)
    totals, features = lax.scan(scan_step, zero_grads, (pixels, feature_grad, live))
    return (features, totals[0], totals[1], totals[2], totals[3], totals[4], totals[5], totals[6], totals[7], totals[8])
```

```python
import jax
import jax.numpy as jnp
import numpy as np
from jax import lax
from jax.experimental import pallas as pl
from jax.experimental.pallas import tpu as pltpu
from jax.sharding import PartitionSpec as P

SIDE = 64
KSIZE = 7
EPS = 1e-06
LANES = 128
CHUNK = 512
PAD = 2
BLOCKS = 8
HALF_PEAK = -0.3257480647361595
EXACT = lax.Precision.HIGHEST
MESH = pl.DeviceIdType.MESH

f32 = jnp.float32
bf16 = jnp.bfloat16


def dot(a, b, dims=((1,), (0,))):
    return lax.dot_general(a, b, (dims, ((), ())), preferred_element_type=f32)


def wide(value, times):
    return jnp.concatenate([value] * times, axis=1)


def fold(value):
    total = value[:, :LANES]
    for at in range(LANES, value.shape[1], LANES):
        total = total + value[:, at : at + LANES]
    return total


def unit(values):
    centre = jnp.mean(values, axis=0, keepdims=True)
    shifted = values - centre
    spread = jnp.mean(jnp.square(shifted), axis=0, keepdims=True)
    scale = lax.rsqrt(spread + EPS)
    return shifted * scale, scale


def gelu_twice(x):
    shape = 1.0 + lax.erf(x * 0.7071067811865476)
    decay = jnp.exp2(x * x * -0.7213475204444817 + HALF_PEAK)
    return x * shape, shape + x * decay


def body(
    count_ref, pix_hbm, grad_hbm, wst_ref, gain_ref, shift_ref, norm_ref, scale_ref, kernel_ref,
    wet_in_ref, bias_ref, wr_ref, place_ref, place_back_ref, pick_ref, feat_hbm, sums_ref, base_s,
    mix_s, pix_v, grad_v, feat_v, par_ref, ws_ref, we_ref, wet_ref, wrt_ref, wrs_ref, taps_ref,
    back_ref, dws_ref, dvec_ref, dwe_ref, dwr_ref, dk_ref, pix_sem, grad_sem, feat_sem,
):
    slots, channels, area = grad_v.shape
    patch = pix_v.shape[1]
    count = count_ref[0]
    pairs = area // LANES
    per = CHUNK // LANES
    chunks = area // CHUNK
    hidden = we_ref.shape[0]
    rows = slots

    def pix_copy(slot):
        return pltpu.make_async_copy(pix_hbm.at[slot], pix_v.at[slot], pix_sem.at[slot])

    def grad_copy(slot):
        return pltpu.make_async_copy(grad_hbm.at[slot], grad_v.at[slot], grad_sem.at[slot])

    def feat_copy(slot, side):
        return pltpu.make_async_copy(feat_v.at[side], feat_hbm.at[slot], feat_sem.at[side])

    @pl.loop(0, count)
    def _(slot):
        pix_copy(slot).start()

    @pl.loop(0, count)
    def _(slot):
        grad_copy(slot).start()

    row_at = lax.broadcasted_iota(jnp.int32, (SIDE, LANES), 0)
    lane_at = lax.broadcasted_iota(jnp.int32, (SIDE, LANES), 1) % SIDE
    near = jnp.abs(row_at - lane_at) <= KSIZE // 2
    row_all = lax.broadcasted_iota(jnp.int32, (LANES, LANES), 0)
    lane_all = lax.broadcasted_iota(jnp.int32, (LANES, LANES), 1)
    same = row_all // SIDE == lane_all // SIDE
    mirror = (same & (row_all % SIDE + lane_all % SIDE == SIDE - 1)).astype(f32).astype(bf16)

    def read(ref, slot, chunk):
        return jnp.concatenate(
            [
                ref[PAD + chunk * per + at, pl.ds(slot, channels, stride=rows), :]
                for at in range(per)
            ],
            axis=1,
        )

    def write(ref, slot, chunk, value):
        for at in range(per):
            ref[PAD + chunk * per + at, pl.ds(slot, channels, stride=rows), :] = value[
                :, at * LANES : (at + 1) * LANES
            ]

    def param(at):
        return wide(par_ref[at], per)

    def toeplitz(ref, c):
        blocks = []
        for m in range(BLOCKS):
            row = jnp.broadcast_to(ref[m, pl.ds(c, 1), :], (SIDE, LANES))
            turned = pltpu.roll(row, 0, 1, stride=1, stride_axis=0)
            blocks.append(jnp.where(near, turned, 0.0).astype(bf16))
        return jnp.concatenate(blocks, axis=0)

    lane_rows = lax.broadcasted_iota(jnp.int32, (pairs * rows, LANES), 1)

    def gathered(ref, c):
        at = pl.multiple_of(c * rows, rows)
        full = ref[:, pl.ds(at, rows), :]
        even = full.reshape((pairs + 2 * PAD) * rows, LANES).astype(bf16)
        odd = full[1 : pairs + 3].reshape((pairs + 2) * rows, LANES).astype(bf16)
        size = pairs * rows
        ends = jnp.where(lane_rows < SIDE, even[4 * rows : 4 * rows + size], even[:size])
        return jnp.concatenate(
            [odd[:size], even[2 * rows : 2 * rows + size], odd[2 * rows : 2 * rows + size], ends],
            axis=1,
        )

    edge = jnp.zeros((PAD, channels * rows, LANES), f32)
    for ref in (base_s, mix_s):
        ref[:PAD] = edge
        ref[PAD + pairs :] = edge
    for ref in (dws_ref, dvec_ref, dwe_ref, dwr_ref):
        ref[...] = jnp.zeros(ref.shape, f32)
    for at, ref in enumerate((gain_ref, shift_ref, norm_ref, scale_ref)):
        par_ref[at] = jnp.transpose(jnp.broadcast_to(ref[...], (LANES, channels)))
    kernel = jnp.transpose(kernel_ref[...]).astype(bf16)
    for m in range(BLOCKS):
        taps_ref[m] = dot(kernel, place_ref[m])
        back_ref[m] = dot(kernel, place_back_ref[m])
    stem = jnp.transpose(wst_ref[...].astype(f32))
    stem = stem - jnp.mean(stem, axis=0, keepdims=True)
    high = stem.astype(bf16)
    ws_ref[:, :patch] = high
    ws_ref[:, patch:] = (stem - high.astype(f32)).astype(bf16)
    weight = wet_in_ref[...].astype(f32) * wide(par_ref[2], hidden // LANES)
    weight = weight - jnp.mean(weight, axis=0, keepdims=True)
    wet_ref[...] = weight.astype(bf16)
    weight = jnp.transpose(weight)
    scaled = wr_ref[...].astype(f32) * (0.5 * wide(par_ref[3], hidden // LANES))
    wrs_ref[...] = scaled.astype(bf16)
    wrt_ref[...] = jnp.transpose(scaled).astype(bf16)
    bias = jnp.transpose(jnp.broadcast_to(bias_ref[...][None], (LANES, hidden)))
    high = bias.astype(bf16).astype(f32)
    middle = (bias - high).astype(bf16).astype(f32)
    low = bias - high - middle
    lane = lax.broadcasted_iota(jnp.int32, (hidden, LANES), 1)
    extra = jnp.where(
        lane == channels,
        high,
        jnp.where(lane == channels + 1, middle, jnp.where(lane == channels + 2, low, 0.0)),
    )
    we_ref[...] = extra.astype(bf16)
    we_ref[:, :channels] = weight.astype(bf16)

    def stem_hat(slot, at):
        pix = pix_v[slot, :, pl.ds(at, CHUNK)]
        out = dot(ws_ref[...], jnp.concatenate([pix, pix], axis=0))
        spread = jnp.mean(jnp.square(out), axis=0, keepdims=True)
        scale = lax.rsqrt(spread + EPS)
        return out * scale, scale, pix

    @pl.loop(0, count)
    def _(slot):
        pix_copy(slot).wait()

        @pl.loop(0, chunks, unroll=4)
        def _(chunk):
            at = pl.multiple_of(chunk * CHUNK, CHUNK)
            hat, _, _ = stem_hat(slot, at)
            write(base_s, slot, chunk, hat * param(0) + param(1))

    @pl.loop(count, slots)
    def _(slot):
        @pl.loop(0, chunks)
        def _(chunk):
            write(base_s, slot, chunk, jnp.zeros((channels, CHUNK), f32))

    @pl.loop(0, channels, unroll=8)
    def _(c):
        out = dot(gathered(base_s, c), toeplitz(taps_ref, c))
        at = pl.multiple_of(c * rows, rows)
        mix_s[PAD : PAD + pairs, pl.ds(at, rows), :] = out.reshape(pairs, rows, LANES)

    @pl.loop(0, count)
    def _(slot):
        side = slot % 2
        grad_copy(slot).wait()

        @pl.when(slot >= 2)
        def _():
            feat_copy(slot, side).wait()

        @pl.loop(0, chunks, unroll=4)
        def _(chunk):
            at = pl.multiple_of(chunk * CHUNK, CHUNK)
            hat, scale = unit(read(mix_s, slot, chunk))
            normed = jnp.concatenate(
                [hat.astype(bf16), jnp.ones((LANES - channels, CHUNK), bf16)], axis=0
            )
            grad = grad_v[slot, :, pl.ds(at, CHUNK)]
            ex = dot(we_ref[...], normed)
            dh = dot(wrt_ref[...], grad)
            acts, slopes = [], []
            for h in range(0, hidden, 16):
                act, slope = gelu_twice(ex[h : h + 16])
                acts.append(act.astype(bf16))
                slopes.append((slope * dh[h : h + 16]).astype(bf16))
            hid = jnp.concatenate(acts, axis=0)
            de = jnp.concatenate(slopes, axis=0)
            reduced = dot(wrs_ref[...], hid)
            feat_v[side, :, pl.ds(at, CHUNK)] = (read(base_s, slot, chunk) + reduced).astype(bf16)
            dwr_ref[...] += dot(grad, hid, ((1,), (1,)))
            dwe_ref[...] += dot(de, normed, ((1,), (1,)))
            dn = dot(wet_ref[...], de)
            second = jnp.mean(dn * hat, axis=0, keepdims=True)
            write(mix_s, slot, chunk, scale * (dn - hat * second))

        feat_copy(slot, side).start()

    @pl.loop(count, slots)
    def _(slot):
        side = slot % 2

        @pl.when(slot >= 2)
        def _():
            feat_copy(slot, side).wait()

        @pl.loop(0, chunks)
        def _(chunk):
            at = pl.multiple_of(chunk * CHUNK, CHUNK)
            feat_v[side, :, pl.ds(at, CHUNK)] = jnp.zeros((channels, CHUNK), bf16)

        feat_copy(slot, side).start()

    lane_one = lax.broadcasted_iota(jnp.int32, (8, LANES), 1)
    lane_half = lane_one % SIDE
    lower = (lane_one >= 3) & (lane_one < SIDE + 3)

    def banded(cross, r, k, turn):
        def tall(v):
            return cross[r * SIDE + 8 * v : r * SIDE + 8 * v + 8, k * LANES : (k + 1) * LANES]

        even = jnp.where(lane_half < 4, 0.0, tall(6))
        for v in (4, 2, 0):
            even = jnp.where(lane_half >= 52 - 8 * v, tall(v), even)
        odd = tall(7)
        for v in (5, 3, 1):
            odd = jnp.where(lane_half >= 52 - 8 * v, tall(v), odd)
        odd = jnp.where(lane_half >= 60, 0.0, odd)
        return pltpu.roll(even, turn, 1, stride=1, stride_axis=0) + pltpu.roll(
            odd, turn + 8, 1, stride=1, stride_axis=0
        )

    @pl.loop(0, channels, unroll=8)
    def _(c):
        at = pl.multiple_of(c * rows, rows)
        grad = mix_s[PAD : PAD + pairs, pl.ds(at, rows), :]
        grad = grad.reshape(pairs * rows, LANES).astype(bf16)
        grad = dot(mirror, grad, ((1,), (1,))).astype(bf16)
        cross = dot(grad, gathered(base_s, c))
        first = [banded(cross, 0, k, 0) for k in (3, 0, 1, 2)]
        second = [banded(cross, 1, k, SIDE) for k in (0, 1, 2, 3)]
        taken = [second[0]] + [
            jnp.where(lower, second[k - 1], second[k]) for k in range(1, 4)
        ]
        for k in range(4):
            dk_ref[k, pl.ds(c, 1), :] = jnp.sum(first[k] + taken[k], axis=0, keepdims=True)
        out = dot(gathered(mix_s, c), toeplitz(back_ref, c))
        mix_s[PAD : PAD + pairs, pl.ds(at, rows), :] = out.reshape(pairs, rows, LANES)

    @pl.loop(0, count)
    def _(slot):
        @pl.loop(0, chunks, unroll=4)
        def _(chunk):
            at = pl.multiple_of(chunk * CHUNK, CHUNK)
            hat, scale, pix = stem_hat(slot, at)
            dbase = grad_v[slot, :, pl.ds(at, CHUNK)].astype(f32) + read(mix_s, slot, chunk)
            turned = dbase * hat
            dvec_ref[0] += fold(turned)
            dvec_ref[1] += fold(dbase)
            scaled = dbase * param(0)
            first = jnp.mean(scaled, axis=0, keepdims=True)
            second = jnp.mean(turned * param(0), axis=0, keepdims=True)
            dstem = (scale * (scaled - first - hat * second)).astype(bf16)
            dws_ref[:, :patch] += dot(dstem, pix, ((1,), (1,)))

    mixed = dws_ref[...]
    for at in range(4):
        mixed += lax.dot_general(
            dk_ref[at], pick_ref[at], (((1,), (0,)), ((), ())), precision=EXACT,
            preferred_element_type=f32,
        )
    products = dwr_ref[...] * 0.5
    expand = jnp.transpose(dwe_ref[...])
    singles = [jnp.sum(dvec_ref[at], axis=1, keepdims=True) for at in range(2)]
    singles.append(
        jnp.sum(expand[:channels] * wet_in_ref[...].astype(f32), axis=1, keepdims=True)
    )
    singles.append(jnp.sum(products * wr_ref[...].astype(f32), axis=1, keepdims=True))
    lane = lax.broadcasted_iota(jnp.int32, (channels, LANES), 1)
    start = first_single(patch)
    for at, single in enumerate(singles):
        mixed = jnp.where(lane == start + at, single, mixed)
    mixed = jnp.concatenate([mixed, jnp.zeros((LANES - channels, LANES), f32)], axis=0)
    top = first_bias(patch)
    sums_ref[:top] = jnp.transpose(mixed)[:top]
    products = products * wide(par_ref[3], hidden // LANES)
    tail = expand[channels : channels + 1]
    expand = expand[:channels] * wide(par_ref[2], hidden // LANES)
    for at in range(hidden // LANES):
        sums_ref[top : top + 1] = tail[:, at * LANES : (at + 1) * LANES]
        top += 1
    for value in (expand, products):
        for at in range(hidden // LANES):
            sums_ref[top : top + channels] = value[:, at * LANES : (at + 1) * LANES]
            top += channels
    if top < sums_ref.shape[0]:
        sums_ref[top:] = jnp.zeros((sums_ref.shape[0] - top, LANES), f32)
    for side in range(min(2, slots)):
        feat_copy(side, side).wait()


def first_single(patch):
    return patch + KSIZE * KSIZE


def first_bias(patch):
    return first_single(patch) + 4


def total_rows(patch, channels, hidden, share):
    blocks = hidden // LANES
    total = first_bias(patch) + blocks + 2 * channels * blocks
    return -(-total // share) * share


def tap_places(patch):
    half = KSIZE // 2
    taps = KSIZE * KSIZE
    place = np.zeros((BLOCKS, taps, LANES), np.float32)
    for at, m in enumerate((2, 3, 4, 5, 6, 7, 8, 1)):
        for r in range(2):
            a = m - 2 * PAD - r
            if abs(a) > half:
                continue
            for b in range(-half, half + 1):
                place[at, (a + half) * KSIZE + b + half, (r * SIDE - b) % LANES] = 1.0
    pick = np.zeros((4, LANES, LANES), np.float32)
    for k in range(4):
        for rr in range(2):
            a = 2 * (k - PAD) + rr
            if abs(a) > half:
                continue
            for b in range(-half, half + 1):
                for step in range(4):
                    lane = (rr * SIDE + SIDE - 1 - 16 * step + b) % LANES
                    pick[k, lane, patch + (a + half) * KSIZE + b + half] = 1.0
    return place, pick


def encode_slots(pixels, feature_grad, count, weights, share=1):
    (ws, stem_gain, stem_shift, kernel, block_gain, we, bias, wr, layer_scale) = weights
    slots, patch, area = pixels.shape
    channels = ws.shape[0]
    hidden = we.shape[0]
    pairs = area // LANES
    place, pick = tap_places(patch)
    total = total_rows(patch, channels, hidden, share)
    consts = (
        ws.T, stem_gain[None], stem_shift[None], block_gain[None], layer_scale[None], kernel.T,
        we.T, bias, wr, jnp.asarray(place, bf16),
        jnp.asarray(place[:, ::-1], bf16), jnp.asarray(pick),
    )
    vmem = pl.BlockSpec(memory_space=pltpu.VMEM)
    hbm = pl.BlockSpec(memory_space=pl.ANY)
    return pl.pallas_call(
        body,
        in_specs=[pl.BlockSpec(memory_space=pltpu.SMEM), hbm, hbm] + [vmem] * len(consts),
        out_specs=[hbm, vmem],
        scratch_shapes=[
            pltpu.VMEM((pairs + 2 * PAD, channels * slots, LANES), f32),
            pltpu.VMEM((pairs + 2 * PAD, channels * slots, LANES), f32),
            pltpu.VMEM((slots, patch, area), bf16),
            pltpu.VMEM((slots, channels, area), bf16),
            pltpu.VMEM((2, channels, area), bf16),
            pltpu.VMEM((4, channels, LANES), f32),
            pltpu.VMEM((channels, 2 * patch), bf16),
            pltpu.VMEM((hidden, LANES), bf16),
            pltpu.VMEM((channels, hidden), bf16),
            pltpu.VMEM((hidden, channels), bf16),
            pltpu.VMEM((channels, hidden), bf16),
            pltpu.VMEM((BLOCKS, channels, LANES), f32),
            pltpu.VMEM((BLOCKS, channels, LANES), f32),
            pltpu.VMEM((channels, LANES), f32),
            pltpu.VMEM((2, channels, LANES), f32),
            pltpu.VMEM((hidden, LANES), f32),
            pltpu.VMEM((channels, hidden), f32),
            pltpu.VMEM((4, channels, LANES), f32),
            pltpu.SemaphoreType.DMA((slots,)),
            pltpu.SemaphoreType.DMA((slots,)),
            pltpu.SemaphoreType.DMA((2,)),
        ],
        out_shape=[
            jax.ShapeDtypeStruct((slots, channels, area), bf16),
            jax.ShapeDtypeStruct((total, LANES), f32),
        ],
        compiler_params=pltpu.CompilerParams(vmem_limit_bytes=60 * 2**20),
    )(count, pixels, feature_grad, *consts)


def add_up(sums_ref, out_ref, outgoing, land_e, land_r, full, out_sems, in_sems):
    count_e = lax.axis_size("enc")
    count_r = lax.axis_size("region")
    me_e = lax.axis_index("enc")
    me_r = lax.axis_index("region")
    barrier = pltpu.get_barrier_semaphore()
    for d in range(1, count_e):
        pl.semaphore_signal(
            barrier, 1, device_id={"enc": lax.rem(me_e + d, count_e)}, device_id_type=MESH
        )
    for d in range(1, count_r):
        pl.semaphore_signal(
            barrier, 1, device_id={"region": lax.rem(me_r + d, count_r)}, device_id_type=MESH
        )
    outgoing[...] = sums_ref[...].astype(bf16)
    pl.semaphore_wait(barrier, count_e + count_r - 2)
    size = land_e.shape[1]
    sems = iter(range(2 * (count_e - 1) + count_r - 1))

    def block(index):
        return pl.ds(pl.multiple_of(index * size, 16), size)

    def exchange(axis, count, me, source, target):
        copies = []
        for d in range(1, count):
            peer = lax.rem(me + d, count)
            sem = next(sems)
            copy = pltpu.make_async_remote_copy(
                src_ref=source(peer), dst_ref=target(d), send_sem=out_sems.at[sem],
                recv_sem=in_sems.at[sem], device_id={axis: peer}, device_id_type=MESH,
            )
            copy.start()
            copies.append(copy)
        for copy in copies:
            copy.wait()

    exchange(
        "enc", count_e, me_e, lambda peer: outgoing.at[block(peer)], lambda d: land_e.at[d - 1]
    )
    value = sums_ref[block(me_e)]
    for d in range(1, count_e):
        value += land_e[d - 1].astype(f32)
    land_r[me_r] = value.astype(bf16)
    mine = land_r.at[me_r]
    exchange("region", count_r, me_r, lambda peer: mine, lambda d: mine)
    value = land_r[0].astype(f32)
    for at in range(1, count_r):
        value += land_r[at].astype(f32)
    full[block(me_e)] = value.astype(bf16)
    own = full.at[block(me_e)]
    exchange("enc", count_e, me_e, lambda peer: own, lambda d: own)
    out_ref[...] = full[...]


def unpack(
    full_ref, stem_ref, gain_ref, shift_ref, kernel_ref, norm_ref, expand_ref, bias_ref, reduce_ref,
    scale_ref,
):
    patch, channels = stem_ref.shape
    hidden = expand_ref.shape[1]
    full = full_ref[...].astype(f32)
    start = first_single(patch)
    stem_ref[...] = full[:patch, :channels]
    kernel_ref[...] = full[patch:start, :channels]
    for at, ref in enumerate((gain_ref, shift_ref, norm_ref, scale_ref)):
        ref[...] = full[start + at : start + at + 1, :channels]
    top = first_bias(patch)
    parts = range(hidden // LANES)
    for at in parts:
        bias_ref[at * LANES : (at + 1) * LANES] = full[top + at]
    top += len(parts)
    for ref in (expand_ref, reduce_ref):
        for at in parts:
            ref[:, at * LANES : (at + 1) * LANES] = full[top : top + channels]
            top += channels


def summed_over_devices(sums, weights):
    (ws, stem_gain, stem_shift, kernel, block_gain, we, bias, wr, layer_scale) = weights
    count_e = lax.axis_size("enc")
    count_r = lax.axis_size("region")
    size = sums.shape[0] // count_e
    copies = 2 * (count_e - 1) + count_r - 1
    vmem = pl.BlockSpec(memory_space=pltpu.VMEM)
    full = pl.pallas_call(
        add_up,
        in_specs=[vmem],
        out_specs=vmem,
        out_shape=jax.ShapeDtypeStruct(sums.shape, bf16),
        scratch_shapes=[
            pltpu.VMEM(sums.shape, bf16),
            pltpu.VMEM((count_e - 1, size, LANES), bf16),
            pltpu.VMEM((count_r, size, LANES), bf16),
            pltpu.VMEM(sums.shape, bf16),
            pltpu.SemaphoreType.DMA((copies,)),
            pltpu.SemaphoreType.DMA((copies,)),
        ],
        compiler_params=pltpu.CompilerParams(collective_id=0, has_side_effects=True),
    )(sums)
    shapes = [
        ws.shape[::-1], (1, stem_gain.shape[0]), (1, stem_shift.shape[0]), kernel.shape[::-1],
        (1, block_gain.shape[0]), we.shape[::-1], bias.shape, wr.shape, (1, layer_scale.shape[0]),
    ]
    outs = pl.pallas_call(
        unpack,
        in_specs=[vmem],
        out_specs=[vmem] * len(shapes),
        out_shape=[jax.ShapeDtypeStruct(shape, f32) for shape in shapes],
    )(full)
    stem, gain, shift, kernel, norm, expand, bias, reduce, scale = outs
    return (
        stem.T, gain[0], shift[0], kernel.T, norm[0], expand.T, bias, reduce, scale[0],
    )


def on_device(pixels, feature_grad, tissue_count, *weights):
    share = 16 * lax.axis_size("enc")
    features, sums = encode_slots(pixels, feature_grad, tissue_count, weights, share)
    return (features, *summed_over_devices(sums, weights))


def solution(mesh):
    return jax.shard_map(
        on_device,
        mesh=mesh,
        in_specs=(
            P(("region", "enc"), None, None),
            P(("region", "enc"), None, None),
            P(("region", "enc")),
        )
        + (P(),) * 9,
        out_specs=(P(("region", "enc"), None, None),) + (P(),) * 9,
        check_vma=False,
    )
```

```python
import jax
import jax.numpy as jnp
import numpy as np
from jax import lax
from jax.experimental import pallas as pl
from jax.experimental.pallas import tpu as pltpu
from jax.sharding import PartitionSpec as P

SIDE = 64
KSIZE = 7
EPS = 1e-06
LANES = 128
CHUNK = 512
PAD = 2
BLOCKS = 8
HALF_PEAK = -0.3257480647361595
EXACT = lax.Precision.HIGHEST
MESH = pl.DeviceIdType.MESH

f32 = jnp.float32
bf16 = jnp.bfloat16


def dot(a, b, dims=((1,), (0,))):
    return lax.dot_general(a, b, (dims, ((), ())), preferred_element_type=f32)


def wide(value, times):
    return jnp.concatenate([value] * times, axis=1)


def fold(value):
    total = value[:, :LANES]
    for at in range(LANES, value.shape[1], LANES):
        total = total + value[:, at : at + LANES]
    return total


def unit(values):
    centre = jnp.mean(values, axis=0, keepdims=True)
    shifted = values - centre
    spread = jnp.mean(jnp.square(shifted), axis=0, keepdims=True)
    scale = lax.rsqrt(spread + EPS)
    return shifted * scale, scale


def gelu_twice(x):
    shape = 1.0 + lax.erf(x * 0.7071067811865476)
    act = (x * shape).astype(bf16)
    x = x.astype(bf16)
    decay = jnp.exp2(x * x * bf16(-0.7213475204444817) + bf16(HALF_PEAK))
    return act, shape.astype(bf16) + x * decay


def body(
    count_ref, pix_hbm, grad_hbm, wst_ref, gain_ref, shift_ref, norm_ref, scale_ref, kernel_ref,
    wet_in_ref, bias_ref, wr_ref, place_ref, place_back_ref, pick_ref, feat_hbm, sums_ref, base_s,
    mix_s, pix_v, grad_v, feat_v, par_ref, ws_ref, we_ref, wet_ref, wrt_ref, wrs_ref, taps_ref,
    back_ref, dws_ref, dvec_ref, dwe_ref, dwr_ref, dk_ref, pix_sem, grad_sem, feat_sem,
):
    slots, channels, area = grad_v.shape
    patch = pix_v.shape[1]
    count = count_ref[0]
    pairs = area // LANES
    per = CHUNK // LANES
    chunks = area // CHUNK
    hidden = we_ref.shape[0]
    rows = slots

    def pix_copy(slot):
        return pltpu.make_async_copy(pix_hbm.at[slot], pix_v.at[slot], pix_sem.at[slot])

    def grad_copy(slot):
        return pltpu.make_async_copy(grad_hbm.at[slot], grad_v.at[slot], grad_sem.at[slot])

    def feat_copy(slot, side):
        return pltpu.make_async_copy(feat_v.at[side], feat_hbm.at[slot], feat_sem.at[side])

    pix_copy(0).start()

    row_at = lax.broadcasted_iota(jnp.int32, (SIDE, LANES), 0)
    lane_at = lax.broadcasted_iota(jnp.int32, (SIDE, LANES), 1) % SIDE
    near = jnp.abs(row_at - lane_at) <= KSIZE // 2
    row_all = lax.broadcasted_iota(jnp.int32, (LANES, LANES), 0)
    lane_all = lax.broadcasted_iota(jnp.int32, (LANES, LANES), 1)
    same = row_all // SIDE == lane_all // SIDE
    mirror = (same & (row_all % SIDE + lane_all % SIDE == SIDE - 1)).astype(f32).astype(bf16)

    def read(ref, slot, chunk):
        return jnp.concatenate(
            [
                ref[PAD + chunk * per + at, pl.ds(slot, channels, stride=rows), :]
                for at in range(per)
            ],
            axis=1,
        )

    def write(ref, slot, chunk, value):
        for at in range(per):
            ref[PAD + chunk * per + at, pl.ds(slot, channels, stride=rows), :] = value[
                :, at * LANES : (at + 1) * LANES
            ]

    def param(at):
        return wide(par_ref[at], per)

    def toeplitz(ref, c):
        blocks = []
        for m in range(BLOCKS):
            row = jnp.broadcast_to(ref[m, pl.ds(c, 1), :], (SIDE, LANES))
            turned = pltpu.roll(row, 0, 1, stride=1, stride_axis=0)
            blocks.append(jnp.where(near, turned, 0.0).astype(bf16))
        return jnp.concatenate(blocks, axis=0)

    lane_rows = lax.broadcasted_iota(jnp.int32, (pairs * rows, LANES), 1)

    def gathered(ref, c):
        at = pl.multiple_of(c * rows, rows)
        full = ref[:, pl.ds(at, rows), :]
        even = full.reshape((pairs + 2 * PAD) * rows, LANES).astype(bf16)
        odd = full[1 : pairs + 3].reshape((pairs + 2) * rows, LANES).astype(bf16)
        size = pairs * rows
        ends = jnp.where(lane_rows < SIDE, even[4 * rows : 4 * rows + size], even[:size])
        return jnp.concatenate(
            [odd[:size], even[2 * rows : 2 * rows + size], odd[2 * rows : 2 * rows + size], ends],
            axis=1,
        )

    edge = jnp.zeros((PAD, channels * rows, LANES), f32)
    for ref in (base_s, mix_s):
        ref[:PAD] = edge
        ref[PAD + pairs :] = edge
    for ref in (dws_ref, dvec_ref, dwe_ref, dwr_ref):
        ref[...] = jnp.zeros(ref.shape, f32)
    for at, ref in enumerate((gain_ref, shift_ref, norm_ref, scale_ref)):
        par_ref[at] = jnp.transpose(jnp.broadcast_to(ref[...], (LANES, channels)))
    kernel = jnp.transpose(kernel_ref[...]).astype(bf16)
    for m in range(BLOCKS):
        taps_ref[m] = dot(kernel, place_ref[m])
        back_ref[m] = dot(kernel, place_back_ref[m])
    stem = jnp.transpose(wst_ref[...].astype(f32))
    stem = stem - jnp.mean(stem, axis=0, keepdims=True)
    high = stem.astype(bf16)
    ws_ref[:, :patch] = high
    ws_ref[:, patch:] = (stem - high.astype(f32)).astype(bf16)
    weight = wet_in_ref[...].astype(f32) * wide(par_ref[2], hidden // LANES)
    weight = weight - jnp.mean(weight, axis=0, keepdims=True)
    wet_ref[...] = weight.astype(bf16)
    weight = jnp.transpose(weight)
    scaled = wr_ref[...].astype(f32) * (0.5 * wide(par_ref[3], hidden // LANES))
    wrs_ref[...] = scaled.astype(bf16)
    wrt_ref[...] = jnp.transpose(scaled).astype(bf16)
    bias = jnp.transpose(jnp.broadcast_to(bias_ref[...][None], (LANES, hidden)))
    high = bias.astype(bf16).astype(f32)
    middle = (bias - high).astype(bf16).astype(f32)
    low = bias - high - middle
    lane = lax.broadcasted_iota(jnp.int32, (hidden, LANES), 1)
    extra = jnp.where(
        lane == channels,
        high,
        jnp.where(lane == channels + 1, middle, jnp.where(lane == channels + 2, low, 0.0)),
    )
    we_ref[...] = extra.astype(bf16)
    we_ref[:, :channels] = weight.astype(bf16)

    def stem_hat(slot, at):
        pix = pix_v[slot, :, pl.ds(at, CHUNK)]
        out = dot(ws_ref[...], jnp.concatenate([pix, pix], axis=0))
        spread = jnp.mean(jnp.square(out), axis=0, keepdims=True)
        scale = lax.rsqrt(spread + EPS)
        return out * scale, scale, pix

    @pl.loop(0, count)
    def _(slot):
        pix_copy(slot).wait()

        @pl.when(slot + 1 < count)
        def _():
            pix_copy(slot + 1).start()

        grad_copy(slot).start()

        @pl.loop(0, chunks, unroll=4)
        def _(chunk):
            at = pl.multiple_of(chunk * CHUNK, CHUNK)
            hat, _, _ = stem_hat(slot, at)
            write(base_s, slot, chunk, hat * param(0) + param(1))

    @pl.loop(count, slots)
    def _(slot):
        @pl.loop(0, chunks)
        def _(chunk):
            write(base_s, slot, chunk, jnp.zeros((channels, CHUNK), f32))

    @pl.loop(0, channels, unroll=16)
    def _(c):
        out = dot(gathered(base_s, c), toeplitz(taps_ref, c))
        at = pl.multiple_of(c * rows, rows)
        mix_s[PAD : PAD + pairs, pl.ds(at, rows), :] = out.reshape(pairs, rows, LANES)

    @pl.loop(0, count)
    def _(slot):
        side = slot % 2
        grad_copy(slot).wait()

        @pl.when(slot >= 2)
        def _():
            feat_copy(slot, side).wait()

        @pl.loop(0, chunks, unroll=8)
        def _(chunk):
            at = pl.multiple_of(chunk * CHUNK, CHUNK)
            hat, scale = unit(read(mix_s, slot, chunk))
            normed = jnp.concatenate(
                [hat.astype(bf16), jnp.ones((LANES - channels, CHUNK), bf16)], axis=0
            )
            grad = grad_v[slot, :, pl.ds(at, CHUNK)]
            ex = dot(we_ref[...], normed)
            dh = dot(wrt_ref[...], grad).astype(bf16)
            acts, slopes = [], []
            for h in range(0, hidden, 16):
                act, slope = gelu_twice(ex[h : h + 16])
                acts.append(act)
                slopes.append(slope * dh[h : h + 16])
            hid = jnp.concatenate(acts, axis=0)
            de = jnp.concatenate(slopes, axis=0)
            reduced = dot(wrs_ref[...], hid)
            feat_v[side, :, pl.ds(at, CHUNK)] = (read(base_s, slot, chunk) + reduced).astype(bf16)
            dwr_ref[:, :channels] += dot(hid, grad, ((1,), (1,)))
            dwe_ref[...] += dot(de, normed, ((1,), (1,)))
            dn = dot(wet_ref[...], de)
            second = jnp.mean(dn * hat, axis=0, keepdims=True)
            write(mix_s, slot, chunk, scale * (dn - hat * second))

        feat_copy(slot, side).start()

    @pl.loop(count, slots)
    def _(slot):
        side = slot % 2

        @pl.when(slot >= 2)
        def _():
            feat_copy(slot, side).wait()

        @pl.loop(0, chunks)
        def _(chunk):
            at = pl.multiple_of(chunk * CHUNK, CHUNK)
            feat_v[side, :, pl.ds(at, CHUNK)] = jnp.zeros((channels, CHUNK), bf16)

        feat_copy(slot, side).start()

    lane_one = lax.broadcasted_iota(jnp.int32, (8, LANES), 1)
    lane_half = lane_one % SIDE
    lower = (lane_one >= 3) & (lane_one < SIDE + 3)

    def banded(cross, r, k, turn):
        def tall(v):
            return cross[r * SIDE + 8 * v : r * SIDE + 8 * v + 8, k * LANES : (k + 1) * LANES]

        even = jnp.where(lane_half < 4, 0.0, tall(6))
        for v in (4, 2, 0):
            even = jnp.where(lane_half >= 52 - 8 * v, tall(v), even)
        odd = tall(7)
        for v in (5, 3, 1):
            odd = jnp.where(lane_half >= 52 - 8 * v, tall(v), odd)
        odd = jnp.where(lane_half >= 60, 0.0, odd)
        return pltpu.roll(even, turn, 1, stride=1, stride_axis=0) + pltpu.roll(
            odd, turn + 8, 1, stride=1, stride_axis=0
        )

    @pl.loop(0, channels, unroll=8)
    def _(c):
        at = pl.multiple_of(c * rows, rows)
        grad = mix_s[PAD : PAD + pairs, pl.ds(at, rows), :]
        grad = grad.reshape(pairs * rows, LANES).astype(bf16)
        grad = dot(mirror, grad, ((1,), (1,))).astype(bf16)
        cross = dot(grad, gathered(base_s, c))
        first = [banded(cross, 0, k, 0) for k in (3, 0, 1, 2)]
        second = [banded(cross, 1, k, SIDE) for k in (0, 1, 2, 3)]
        taken = [second[0]] + [
            jnp.where(lower, second[k - 1], second[k]) for k in range(1, 4)
        ]
        for k in range(4):
            dk_ref[k, pl.ds(c, 1), :] = jnp.sum(first[k] + taken[k], axis=0, keepdims=True)
        out = dot(gathered(mix_s, c), toeplitz(back_ref, c))
        mix_s[PAD : PAD + pairs, pl.ds(at, rows), :] = out.reshape(pairs, rows, LANES)

    @pl.loop(0, count)
    def _(slot):
        @pl.loop(0, chunks, unroll=4)
        def _(chunk):
            at = pl.multiple_of(chunk * CHUNK, CHUNK)
            hat, scale, pix = stem_hat(slot, at)
            dbase = grad_v[slot, :, pl.ds(at, CHUNK)].astype(f32) + read(mix_s, slot, chunk)
            dvec_ref[...] += fold(dbase)
            second = jnp.mean(dbase * hat * param(0), axis=0, keepdims=True)
            straight = (scale * dbase).astype(bf16)
            along = (hat * (scale * second)).astype(bf16)
            both = dot(jnp.concatenate([straight, along], axis=0), pix, ((1,), (1,)))
            dws_ref[:, :, :patch] += both.reshape(2, channels, patch)

    mixed = dws_ref[0] * par_ref[0] - dws_ref[1]
    mixed = mixed - jnp.mean(mixed, axis=0, keepdims=True)
    for at in range(4):
        mixed += lax.dot_general(
            dk_ref[at], pick_ref[at], (((1,), (0,)), ((), ())), precision=EXACT,
            preferred_element_type=f32,
        )
    products = jnp.transpose(dwr_ref[...])[:channels] * 0.5
    expand = jnp.transpose(dwe_ref[...])
    stem = ws_ref[:, :patch].astype(f32) + ws_ref[:, patch:].astype(f32)
    singles = [
        jnp.sum(dws_ref[0, :, :patch] * stem, axis=1, keepdims=True),
        jnp.sum(dvec_ref[...], axis=1, keepdims=True),
    ]
    singles.append(
        jnp.sum(expand[:channels] * wet_in_ref[...].astype(f32), axis=1, keepdims=True)
    )
    singles.append(jnp.sum(products * wr_ref[...].astype(f32), axis=1, keepdims=True))
    lane = lax.broadcasted_iota(jnp.int32, (channels, LANES), 1)
    start = first_single(patch)
    for at, single in enumerate(singles):
        mixed = jnp.where(lane == start + at, single, mixed)
    mixed = jnp.concatenate([mixed, jnp.zeros((LANES - channels, LANES), f32)], axis=0)
    top = first_bias(patch)
    sums_ref[:top] = jnp.transpose(mixed)[:top]
    products = products * wide(par_ref[3], hidden // LANES)
    tail = expand[channels : channels + 1]
    expand = expand[:channels] * wide(par_ref[2], hidden // LANES)
    for at in range(hidden // LANES):
        sums_ref[top : top + 1] = tail[:, at * LANES : (at + 1) * LANES]
        top += 1
    for value in (expand, products):
        for at in range(hidden // LANES):
            sums_ref[top : top + channels] = value[:, at * LANES : (at + 1) * LANES]
            top += channels
    if top < sums_ref.shape[0]:
        sums_ref[top:] = jnp.zeros((sums_ref.shape[0] - top, LANES), f32)
    for side in range(min(2, slots)):
        feat_copy(side, side).wait()


def first_single(patch):
    return patch + KSIZE * KSIZE


def first_bias(patch):
    return first_single(patch) + 4


def total_rows(patch, channels, hidden, share):
    blocks = hidden // LANES
    total = first_bias(patch) + blocks + 2 * channels * blocks
    return -(-total // share) * share


def tap_places(patch):
    half = KSIZE // 2
    taps = KSIZE * KSIZE
    place = np.zeros((BLOCKS, taps, LANES), np.float32)
    for at, m in enumerate((2, 3, 4, 5, 6, 7, 8, 1)):
        for r in range(2):
            a = m - 2 * PAD - r
            if abs(a) > half:
                continue
            for b in range(-half, half + 1):
                place[at, (a + half) * KSIZE + b + half, (r * SIDE - b) % LANES] = 1.0
    pick = np.zeros((4, LANES, LANES), np.float32)
    for k in range(4):
        for rr in range(2):
            a = 2 * (k - PAD) + rr
            if abs(a) > half:
                continue
            for b in range(-half, half + 1):
                for step in range(4):
                    lane = (rr * SIDE + SIDE - 1 - 16 * step + b) % LANES
                    pick[k, lane, patch + (a + half) * KSIZE + b + half] = 1.0
    return place, pick


def encode_slots(pixels, feature_grad, count, weights, share=1):
    (ws, stem_gain, stem_shift, kernel, block_gain, we, bias, wr, layer_scale) = weights
    slots, patch, area = pixels.shape
    channels = ws.shape[0]
    hidden = we.shape[0]
    pairs = area // LANES
    place, pick = tap_places(patch)
    total = total_rows(patch, channels, hidden, share)
    consts = (
        ws.T, stem_gain[None], stem_shift[None], block_gain[None], layer_scale[None], kernel.T,
        we.T, bias, wr, jnp.asarray(place, bf16),
        jnp.asarray(place[:, ::-1], bf16), jnp.asarray(pick),
    )
    vmem = pl.BlockSpec(memory_space=pltpu.VMEM)
    hbm = pl.BlockSpec(memory_space=pl.ANY)
    return pl.pallas_call(
        body,
        in_specs=[pl.BlockSpec(memory_space=pltpu.SMEM), hbm, hbm] + [vmem] * len(consts),
        out_specs=[hbm, vmem],
        scratch_shapes=[
            pltpu.VMEM((pairs + 2 * PAD, channels * slots, LANES), f32),
            pltpu.VMEM((pairs + 2 * PAD, channels * slots, LANES), f32),
            pltpu.VMEM((slots, patch, area), bf16),
            pltpu.VMEM((slots, channels, area), bf16),
            pltpu.VMEM((2, channels, area), bf16),
            pltpu.VMEM((4, channels, LANES), f32),
            pltpu.VMEM((channels, 2 * patch), bf16),
            pltpu.VMEM((hidden, LANES), bf16),
            pltpu.VMEM((channels, hidden), bf16),
            pltpu.VMEM((hidden, channels), bf16),
            pltpu.VMEM((channels, hidden), bf16),
            pltpu.VMEM((BLOCKS, channels, LANES), f32),
            pltpu.VMEM((BLOCKS, channels, LANES), f32),
            pltpu.VMEM((2, channels, LANES), f32),
            pltpu.VMEM((channels, LANES), f32),
            pltpu.VMEM((hidden, LANES), f32),
            pltpu.VMEM((hidden, LANES), f32),
            pltpu.VMEM((4, channels, LANES), f32),
            pltpu.SemaphoreType.DMA((slots,)),
            pltpu.SemaphoreType.DMA((slots,)),
            pltpu.SemaphoreType.DMA((2,)),
        ],
        out_shape=[
            jax.ShapeDtypeStruct((slots, channels, area), bf16),
            jax.ShapeDtypeStruct((total, LANES), f32),
        ],
        compiler_params=pltpu.CompilerParams(vmem_limit_bytes=60 * 2**20),
    )(count, pixels, feature_grad, *consts)


def add_up(sums_ref, out_ref, outgoing, land_e, land_r, full, out_sems, in_sems):
    count_e = lax.axis_size("enc")
    count_r = lax.axis_size("region")
    me_e = lax.axis_index("enc")
    me_r = lax.axis_index("region")
    barrier = pltpu.get_barrier_semaphore()
    for d in range(1, count_e):
        pl.semaphore_signal(
            barrier, 1, device_id={"enc": lax.rem(me_e + d, count_e)}, device_id_type=MESH
        )
    for d in range(1, count_r):
        pl.semaphore_signal(
            barrier, 1, device_id={"region": lax.rem(me_r + d, count_r)}, device_id_type=MESH
        )
    outgoing[...] = sums_ref[...].astype(bf16)
    pl.semaphore_wait(barrier, count_e + count_r - 2)
    size = land_e.shape[1]
    sems = iter(range(2 * (count_e - 1) + count_r - 1))

    def block(index):
        return pl.ds(pl.multiple_of(index * size, 16), size)

    def exchange(axis, count, me, source, target):
        copies = []
        for d in range(1, count):
            peer = lax.rem(me + d, count)
            sem = next(sems)
            copy = pltpu.make_async_remote_copy(
                src_ref=source(peer), dst_ref=target(d), send_sem=out_sems.at[sem],
                recv_sem=in_sems.at[sem], device_id={axis: peer}, device_id_type=MESH,
            )
            copy.start()
            copies.append(copy)
        for copy in copies:
            copy.wait()

    exchange(
        "enc", count_e, me_e, lambda peer: outgoing.at[block(peer)], lambda d: land_e.at[d - 1]
    )
    value = sums_ref[block(me_e)]
    for d in range(1, count_e):
        value += land_e[d - 1].astype(f32)
    land_r[me_r] = value.astype(bf16)
    mine = land_r.at[me_r]
    exchange("region", count_r, me_r, lambda peer: mine, lambda d: mine)
    value = land_r[0].astype(f32)
    for at in range(1, count_r):
        value += land_r[at].astype(f32)
    full[block(me_e)] = value.astype(bf16)
    own = full.at[block(me_e)]
    exchange("enc", count_e, me_e, lambda peer: own, lambda d: own)
    out_ref[...] = full[...]


def unpack(
    full_ref, stem_ref, gain_ref, shift_ref, kernel_ref, norm_ref, expand_ref, bias_ref, reduce_ref,
    scale_ref,
):
    patch, channels = stem_ref.shape
    hidden = expand_ref.shape[1]
    full = full_ref[...].astype(f32)
    start = first_single(patch)
    stem_ref[...] = full[:patch, :channels]
    kernel_ref[...] = full[patch:start, :channels]
    for at, ref in enumerate((gain_ref, shift_ref, norm_ref, scale_ref)):
        ref[...] = full[start + at : start + at + 1, :channels]
    top = first_bias(patch)
    parts = range(hidden // LANES)
    for at in parts:
        bias_ref[at * LANES : (at + 1) * LANES] = full[top + at]
    top += len(parts)
    for ref in (expand_ref, reduce_ref):
        for at in parts:
            ref[:, at * LANES : (at + 1) * LANES] = full[top : top + channels]
            top += channels


def summed_over_devices(sums, weights):
    (ws, stem_gain, stem_shift, kernel, block_gain, we, bias, wr, layer_scale) = weights
    count_e = lax.axis_size("enc")
    count_r = lax.axis_size("region")
    size = sums.shape[0] // count_e
    copies = 2 * (count_e - 1) + count_r - 1
    vmem = pl.BlockSpec(memory_space=pltpu.VMEM)
    full = pl.pallas_call(
        add_up,
        in_specs=[vmem],
        out_specs=vmem,
        out_shape=jax.ShapeDtypeStruct(sums.shape, bf16),
        scratch_shapes=[
            pltpu.VMEM(sums.shape, bf16),
            pltpu.VMEM((count_e - 1, size, LANES), bf16),
            pltpu.VMEM((count_r, size, LANES), bf16),
            pltpu.VMEM(sums.shape, bf16),
            pltpu.SemaphoreType.DMA((copies,)),
            pltpu.SemaphoreType.DMA((copies,)),
        ],
        compiler_params=pltpu.CompilerParams(collective_id=0, has_side_effects=True),
    )(sums)
    shapes = [
        ws.shape[::-1], (1, stem_gain.shape[0]), (1, stem_shift.shape[0]), kernel.shape[::-1],
        (1, block_gain.shape[0]), we.shape[::-1], bias.shape, wr.shape, (1, layer_scale.shape[0]),
    ]
    outs = pl.pallas_call(
        unpack,
        in_specs=[vmem],
        out_specs=[vmem] * len(shapes),
        out_shape=[jax.ShapeDtypeStruct(shape, f32) for shape in shapes],
    )(full)
    stem, gain, shift, kernel, norm, expand, bias, reduce, scale = outs
    return (
        stem.T, gain[0], shift[0], kernel.T, norm[0], expand.T, bias, reduce, scale[0],
    )


def on_device(pixels, feature_grad, tissue_count, *weights):
    share = 16 * lax.axis_size("enc")
    features, sums = encode_slots(pixels, feature_grad, tissue_count, weights, share)
    return (features, *summed_over_devices(sums, weights))


def solution(mesh):
    return jax.shard_map(
        on_device,
        mesh=mesh,
        in_specs=(
            P(("region", "enc"), None, None),
            P(("region", "enc"), None, None),
            P(("region", "enc")),
        )
        + (P(),) * 9,
        out_specs=(P(("region", "enc"), None, None),) + (P(),) * 9,
        check_vma=False,
    )
```

```python
import jax
import jax.numpy as jnp
import numpy as np
from jax import lax
from jax.experimental import pallas as pl
from jax.experimental.pallas import tpu as pltpu
from jax.sharding import PartitionSpec as P

SIDE = 64
KSIZE = 7
EPS = 1e-06
LANES = 128
CHUNK = 512
PAD = 2
BLOCKS = 8
HALF_PEAK = -0.3257480647361595
EXACT = lax.Precision.HIGHEST
MESH = pl.DeviceIdType.MESH

f32 = jnp.float32
bf16 = jnp.bfloat16


def dot(a, b, dims=((1,), (0,))):
    return lax.dot_general(a, b, (dims, ((), ())), preferred_element_type=f32)


def wide(value, times):
    return jnp.concatenate([value] * times, axis=1)


def fold(value):
    total = value[:, :LANES]
    for at in range(LANES, value.shape[1], LANES):
        total = total + value[:, at : at + LANES]
    return total


def unit(values):
    centre = jnp.mean(values, axis=0, keepdims=True)
    shifted = values - centre
    spread = jnp.mean(jnp.square(shifted), axis=0, keepdims=True)
    scale = lax.rsqrt(spread + EPS)
    return shifted * scale, scale


def gelu_twice(x):
    shape = 1.0 + lax.erf(x * 0.7071067811865476)
    shape = shape.astype(bf16)
    x = x.astype(bf16)
    decay = jnp.exp2(x * x * bf16(-0.7213475204444817) + bf16(HALF_PEAK))
    return x * shape, shape + x * decay


def body(
    count_ref, pix_hbm, grad_hbm, wst_ref, gain_ref, shift_ref, norm_ref, scale_ref, kernel_ref,
    wet_in_ref, bias_ref, wr_ref, place_ref, place_back_ref, pick_ref, feat_hbm, sums_ref, base_s,
    mix_s, pix_v, grad_v, feat_v, par_ref, ws_ref, we_ref, wet_ref, wrt_ref, wrs_ref, taps_ref,
    back_ref, dws_ref, dvec_ref, dwe_ref, dwr_ref, dk_ref, pix_sem, grad_sem, feat_sem,
):
    slots, channels, area = grad_v.shape
    patch = pix_v.shape[1]
    count = count_ref[0]
    pairs = area // LANES
    per = CHUNK // LANES
    chunks = area // CHUNK
    hidden = we_ref.shape[0]
    rows = slots

    def pix_copy(slot):
        return pltpu.make_async_copy(pix_hbm.at[slot], pix_v.at[slot], pix_sem.at[slot])

    def grad_copy(slot):
        return pltpu.make_async_copy(grad_hbm.at[slot], grad_v.at[slot], grad_sem.at[slot])

    def feat_copy(slot, side):
        return pltpu.make_async_copy(feat_v.at[side], feat_hbm.at[slot], feat_sem.at[side])

    pix_copy(0).start()

    row_at = lax.broadcasted_iota(jnp.int32, (SIDE, LANES), 0)
    lane_at = lax.broadcasted_iota(jnp.int32, (SIDE, LANES), 1) % SIDE
    near = jnp.abs(row_at - lane_at) <= KSIZE // 2
    row_all = lax.broadcasted_iota(jnp.int32, (LANES, LANES), 0)
    lane_all = lax.broadcasted_iota(jnp.int32, (LANES, LANES), 1)
    same = row_all // SIDE == lane_all // SIDE
    mirror = (same & (row_all % SIDE + lane_all % SIDE == SIDE - 1)).astype(f32).astype(bf16)

    def read(ref, slot, chunk):
        return jnp.concatenate(
            [
                ref[PAD + chunk * per + at, pl.ds(slot, channels, stride=rows), :]
                for at in range(per)
            ],
            axis=1,
        )

    def write(ref, slot, chunk, value):
        for at in range(per):
            ref[PAD + chunk * per + at, pl.ds(slot, channels, stride=rows), :] = value[
                :, at * LANES : (at + 1) * LANES
            ]

    def param(at):
        return wide(par_ref[at], per)

    def toeplitz(ref, c):
        blocks = []
        for m in range(BLOCKS):
            row = jnp.broadcast_to(ref[m, pl.ds(c, 1), :], (SIDE, LANES))
            turned = pltpu.roll(row, 0, 1, stride=1, stride_axis=0)
            blocks.append(jnp.where(near, turned, 0.0).astype(bf16))
        return jnp.concatenate(blocks, axis=0)

    lane_rows = lax.broadcasted_iota(jnp.int32, (pairs * rows, LANES), 1)

    def gathered(ref, c):
        at = pl.multiple_of(c * rows, rows)
        full = ref[:, pl.ds(at, rows), :]
        even = full.reshape((pairs + 2 * PAD) * rows, LANES).astype(bf16)
        odd = full[1 : pairs + 3].reshape((pairs + 2) * rows, LANES).astype(bf16)
        size = pairs * rows
        ends = jnp.where(lane_rows < SIDE, even[4 * rows : 4 * rows + size], even[:size])
        return jnp.concatenate(
            [odd[:size], even[2 * rows : 2 * rows + size], odd[2 * rows : 2 * rows + size], ends],
            axis=1,
        )

    edge = jnp.zeros((PAD, channels * rows, LANES), f32)
    for ref in (base_s, mix_s):
        ref[:PAD] = edge
        ref[PAD + pairs :] = edge
    for ref in (dws_ref, dvec_ref, dwe_ref, dwr_ref):
        ref[...] = jnp.zeros(ref.shape, f32)
    for at, ref in enumerate((gain_ref, shift_ref, norm_ref, scale_ref)):
        par_ref[at] = jnp.transpose(jnp.broadcast_to(ref[...], (LANES, channels)))
    kernel = jnp.transpose(kernel_ref[...]).astype(bf16)
    for m in range(BLOCKS):
        taps_ref[m] = dot(kernel, place_ref[m])
        back_ref[m] = dot(kernel, place_back_ref[m])
    stem = jnp.transpose(wst_ref[...].astype(f32))
    stem = stem - jnp.mean(stem, axis=0, keepdims=True)
    high = stem.astype(bf16)
    ws_ref[:, :patch] = high
    ws_ref[:, patch:] = (stem - high.astype(f32)).astype(bf16)
    weight = wet_in_ref[...].astype(f32) * wide(par_ref[2], hidden // LANES)
    weight = weight - jnp.mean(weight, axis=0, keepdims=True)
    wet_ref[...] = weight.astype(bf16)
    weight = jnp.transpose(weight)
    scaled = wr_ref[...].astype(f32) * (0.5 * wide(par_ref[3], hidden // LANES))
    wrs_ref[...] = scaled.astype(bf16)
    wrt_ref[...] = jnp.transpose(scaled).astype(bf16)
    bias = jnp.transpose(jnp.broadcast_to(bias_ref[...][None], (LANES, hidden)))
    high = bias.astype(bf16).astype(f32)
    middle = (bias - high).astype(bf16).astype(f32)
    low = bias - high - middle
    lane = lax.broadcasted_iota(jnp.int32, (hidden, LANES), 1)
    extra = jnp.where(
        lane == channels,
        high,
        jnp.where(lane == channels + 1, middle, jnp.where(lane == channels + 2, low, 0.0)),
    )
    we_ref[...] = extra.astype(bf16)
    we_ref[:, :channels] = weight.astype(bf16)

    def stem_hat(slot, at):
        pix = pix_v[slot, :, pl.ds(at, CHUNK)]
        out = dot(ws_ref[...], jnp.concatenate([pix, pix], axis=0))
        spread = jnp.mean(jnp.square(out), axis=0, keepdims=True)
        scale = lax.rsqrt(spread + EPS)
        return out * scale, scale, pix

    @pl.loop(0, count)
    def _(slot):
        pix_copy(slot).wait()

        @pl.when(slot + 1 < count)
        def _():
            pix_copy(slot + 1).start()

        grad_copy(slot).start()

        @pl.loop(0, chunks, unroll=8)
        def _(chunk):
            at = pl.multiple_of(chunk * CHUNK, CHUNK)
            hat, _, _ = stem_hat(slot, at)
            write(base_s, slot, chunk, hat * param(0) + param(1))

    @pl.loop(count, slots)
    def _(slot):
        @pl.loop(0, chunks)
        def _(chunk):
            write(base_s, slot, chunk, jnp.zeros((channels, CHUNK), f32))

    @pl.loop(0, channels, unroll=16)
    def _(c):
        out = dot(gathered(base_s, c), toeplitz(taps_ref, c))
        at = pl.multiple_of(c * rows, rows)
        mix_s[PAD : PAD + pairs, pl.ds(at, rows), :] = out.reshape(pairs, rows, LANES)

    @pl.loop(0, count)
    def _(slot):
        side = slot % 2
        grad_copy(slot).wait()

        @pl.when(slot >= 2)
        def _():
            feat_copy(slot, side).wait()

        @pl.loop(0, chunks, unroll=8)
        def _(chunk):
            at = pl.multiple_of(chunk * CHUNK, CHUNK)
            hat, scale = unit(read(mix_s, slot, chunk))
            normed = jnp.concatenate(
                [hat.astype(bf16), jnp.ones((LANES - channels, CHUNK), bf16)], axis=0
            )
            grad = grad_v[slot, :, pl.ds(at, CHUNK)]
            ex = dot(we_ref[...], normed)
            dh = dot(wrt_ref[...], grad).astype(bf16)
            acts, slopes = [], []
            for h in range(0, hidden, 16):
                act, slope = gelu_twice(ex[h : h + 16])
                acts.append(act)
                slopes.append(slope * dh[h : h + 16])
            hid = jnp.concatenate(acts, axis=0)
            de = jnp.concatenate(slopes, axis=0)
            reduced = dot(wrs_ref[...], hid)
            feat_v[side, :, pl.ds(at, CHUNK)] = (read(base_s, slot, chunk) + reduced).astype(bf16)
            dwr_ref[:, :channels] += dot(hid, grad, ((1,), (1,)))
            dwe_ref[...] += dot(de, normed, ((1,), (1,)))
            dn = dot(wet_ref[...], de)
            second = jnp.mean(dn * hat, axis=0, keepdims=True)
            write(mix_s, slot, chunk, scale * (dn - hat * second))

        feat_copy(slot, side).start()

    @pl.loop(count, slots)
    def _(slot):
        side = slot % 2

        @pl.when(slot >= 2)
        def _():
            feat_copy(slot, side).wait()

        @pl.loop(0, chunks)
        def _(chunk):
            at = pl.multiple_of(chunk * CHUNK, CHUNK)
            feat_v[side, :, pl.ds(at, CHUNK)] = jnp.zeros((channels, CHUNK), bf16)

        feat_copy(slot, side).start()

    lane_one = lax.broadcasted_iota(jnp.int32, (8, LANES), 1)
    lane_half = lane_one % SIDE
    lower = (lane_one >= 3) & (lane_one < SIDE + 3)

    def banded(cross, r, k, turn):
        def tall(v):
            return cross[r * SIDE + 8 * v : r * SIDE + 8 * v + 8, k * LANES : (k + 1) * LANES]

        even = jnp.where(lane_half < 4, 0.0, tall(6))
        for v in (4, 2, 0):
            even = jnp.where(lane_half >= 52 - 8 * v, tall(v), even)
        odd = tall(7)
        for v in (5, 3, 1):
            odd = jnp.where(lane_half >= 52 - 8 * v, tall(v), odd)
        odd = jnp.where(lane_half >= 60, 0.0, odd)
        return pltpu.roll(even, turn, 1, stride=1, stride_axis=0) + pltpu.roll(
            odd, turn + 8, 1, stride=1, stride_axis=0
        )

    @pl.loop(0, channels, unroll=8)
    def _(c):
        at = pl.multiple_of(c * rows, rows)
        grad = mix_s[PAD : PAD + pairs, pl.ds(at, rows), :]
        grad = grad.reshape(pairs * rows, LANES).astype(bf16)
        grad = dot(mirror, grad, ((1,), (1,))).astype(bf16)
        cross = dot(grad, gathered(base_s, c))
        first = [banded(cross, 0, k, 0) for k in (3, 0, 1, 2)]
        second = [banded(cross, 1, k, SIDE) for k in (0, 1, 2, 3)]
        taken = [second[0]] + [
            jnp.where(lower, second[k - 1], second[k]) for k in range(1, 4)
        ]
        for k in range(4):
            dk_ref[k, pl.ds(c, 1), :] = jnp.sum(first[k] + taken[k], axis=0, keepdims=True)
        out = dot(gathered(mix_s, c), toeplitz(back_ref, c))
        mix_s[PAD : PAD + pairs, pl.ds(at, rows), :] = out.reshape(pairs, rows, LANES)

    @pl.loop(0, count)
    def _(slot):
        @pl.loop(0, chunks, unroll=4)
        def _(chunk):
            at = pl.multiple_of(chunk * CHUNK, CHUNK)
            hat, scale, pix = stem_hat(slot, at)
            dbase = grad_v[slot, :, pl.ds(at, CHUNK)].astype(f32) + read(mix_s, slot, chunk)
            dvec_ref[...] += fold(dbase)
            second = jnp.mean(dbase * hat * param(0), axis=0, keepdims=True)
            straight = (scale * dbase).astype(bf16)
            along = (hat * (scale * second)).astype(bf16)
            both = dot(jnp.concatenate([straight, along], axis=0), pix, ((1,), (1,)))
            dws_ref[:, :, :patch] += both.reshape(2, channels, patch)

    mixed = dws_ref[0] * par_ref[0] - dws_ref[1]
    mixed = mixed - jnp.mean(mixed, axis=0, keepdims=True)
    for at in range(4):
        mixed += lax.dot_general(
            dk_ref[at], pick_ref[at], (((1,), (0,)), ((), ())), precision=EXACT,
            preferred_element_type=f32,
        )
    products = jnp.transpose(dwr_ref[...])[:channels] * 0.5
    expand = jnp.transpose(dwe_ref[...])
    stem = ws_ref[:, :patch].astype(f32) + ws_ref[:, patch:].astype(f32)
    singles = [
        jnp.sum(dws_ref[0, :, :patch] * stem, axis=1, keepdims=True),
        jnp.sum(dvec_ref[...], axis=1, keepdims=True),
    ]
    singles.append(
        jnp.sum(expand[:channels] * wet_in_ref[...].astype(f32), axis=1, keepdims=True)
    )
    singles.append(jnp.sum(products * wr_ref[...].astype(f32), axis=1, keepdims=True))
    lane = lax.broadcasted_iota(jnp.int32, (channels, LANES), 1)
    start = first_single(patch)
    for at, single in enumerate(singles):
        mixed = jnp.where(lane == start + at, single, mixed)
    mixed = jnp.concatenate([mixed, jnp.zeros((LANES - channels, LANES), f32)], axis=0)
    top = first_bias(patch)
    sums_ref[:top] = jnp.transpose(mixed)[:top]
    products = products * wide(par_ref[3], hidden // LANES)
    tail = expand[channels : channels + 1]
    expand = expand[:channels] * wide(par_ref[2], hidden // LANES)
    for at in range(hidden // LANES):
        sums_ref[top : top + 1] = tail[:, at * LANES : (at + 1) * LANES]
        top += 1
    for value in (expand, products):
        for at in range(hidden // LANES):
            sums_ref[top : top + channels] = value[:, at * LANES : (at + 1) * LANES]
            top += channels
    if top < sums_ref.shape[0]:
        sums_ref[top:] = jnp.zeros((sums_ref.shape[0] - top, LANES), f32)
    for side in range(min(2, slots)):
        feat_copy(side, side).wait()


def first_single(patch):
    return patch + KSIZE * KSIZE


def first_bias(patch):
    return first_single(patch) + 4


def total_rows(patch, channels, hidden, share):
    blocks = hidden // LANES
    total = first_bias(patch) + blocks + 2 * channels * blocks
    return -(-total // share) * share


def tap_places(patch):
    half = KSIZE // 2
    taps = KSIZE * KSIZE
    place = np.zeros((BLOCKS, taps, LANES), np.float32)
    for at, m in enumerate((2, 3, 4, 5, 6, 7, 8, 1)):
        for r in range(2):
            a = m - 2 * PAD - r
            if abs(a) > half:
                continue
            for b in range(-half, half + 1):
                place[at, (a + half) * KSIZE + b + half, (r * SIDE - b) % LANES] = 1.0
    pick = np.zeros((4, LANES, LANES), np.float32)
    for k in range(4):
        for rr in range(2):
            a = 2 * (k - PAD) + rr
            if abs(a) > half:
                continue
            for b in range(-half, half + 1):
                for step in range(4):
                    lane = (rr * SIDE + SIDE - 1 - 16 * step + b) % LANES
                    pick[k, lane, patch + (a + half) * KSIZE + b + half] = 1.0
    return place, pick


def encode_slots(pixels, feature_grad, count, weights, share=1):
    (ws, stem_gain, stem_shift, kernel, block_gain, we, bias, wr, layer_scale) = weights
    slots, patch, area = pixels.shape
    channels = ws.shape[0]
    hidden = we.shape[0]
    pairs = area // LANES
    place, pick = tap_places(patch)
    total = total_rows(patch, channels, hidden, share)
    consts = (
        ws.T, stem_gain[None], stem_shift[None], block_gain[None], layer_scale[None], kernel.T,
        we.T, bias, wr, jnp.asarray(place, bf16),
        jnp.asarray(place[:, ::-1], bf16), jnp.asarray(pick),
    )
    vmem = pl.BlockSpec(memory_space=pltpu.VMEM)
    hbm = pl.BlockSpec(memory_space=pl.ANY)
    return pl.pallas_call(
        body,
        in_specs=[pl.BlockSpec(memory_space=pltpu.SMEM), hbm, hbm] + [vmem] * len(consts),
        out_specs=[hbm, vmem],
        scratch_shapes=[
            pltpu.VMEM((pairs + 2 * PAD, channels * slots, LANES), f32),
            pltpu.VMEM((pairs + 2 * PAD, channels * slots, LANES), f32),
            pltpu.VMEM((slots, patch, area), bf16),
            pltpu.VMEM((slots, channels, area), bf16),
            pltpu.VMEM((2, channels, area), bf16),
            pltpu.VMEM((4, channels, LANES), f32),
            pltpu.VMEM((channels, 2 * patch), bf16),
            pltpu.VMEM((hidden, LANES), bf16),
            pltpu.VMEM((channels, hidden), bf16),
            pltpu.VMEM((hidden, channels), bf16),
            pltpu.VMEM((channels, hidden), bf16),
            pltpu.VMEM((BLOCKS, channels, LANES), f32),
            pltpu.VMEM((BLOCKS, channels, LANES), f32),
            pltpu.VMEM((2, channels, LANES), f32),
            pltpu.VMEM((channels, LANES), f32),
            pltpu.VMEM((hidden, LANES), f32),
            pltpu.VMEM((hidden, LANES), f32),
            pltpu.VMEM((4, channels, LANES), f32),
            pltpu.SemaphoreType.DMA((slots,)),
            pltpu.SemaphoreType.DMA((slots,)),
            pltpu.SemaphoreType.DMA((2,)),
        ],
        out_shape=[
            jax.ShapeDtypeStruct((slots, channels, area), bf16),
            jax.ShapeDtypeStruct((total, LANES), f32),
        ],
        compiler_params=pltpu.CompilerParams(vmem_limit_bytes=60 * 2**20),
    )(count, pixels, feature_grad, *consts)


def add_up(sums_ref, out_ref, outgoing, land_e, land_r, full, out_sems, in_sems):
    count_e = lax.axis_size("enc")
    count_r = lax.axis_size("region")
    me_e = lax.axis_index("enc")
    me_r = lax.axis_index("region")
    barrier = pltpu.get_barrier_semaphore()
    for d in range(1, count_e):
        pl.semaphore_signal(
            barrier, 1, device_id={"enc": lax.rem(me_e + d, count_e)}, device_id_type=MESH
        )
    for d in range(1, count_r):
        pl.semaphore_signal(
            barrier, 1, device_id={"region": lax.rem(me_r + d, count_r)}, device_id_type=MESH
        )
    outgoing[...] = sums_ref[...].astype(bf16)
    pl.semaphore_wait(barrier, count_e + count_r - 2)
    size = land_e.shape[1]
    sems = iter(range(2 * (count_e - 1) + count_r - 1))

    def block(index):
        return pl.ds(pl.multiple_of(index * size, 16), size)

    def exchange(axis, count, me, source, target):
        copies = []
        for d in range(1, count):
            peer = lax.rem(me + d, count)
            sem = next(sems)
            copy = pltpu.make_async_remote_copy(
                src_ref=source(peer), dst_ref=target(d), send_sem=out_sems.at[sem],
                recv_sem=in_sems.at[sem], device_id={axis: peer}, device_id_type=MESH,
            )
            copy.start()
            copies.append(copy)
        for copy in copies:
            copy.wait()

    exchange(
        "enc", count_e, me_e, lambda peer: outgoing.at[block(peer)], lambda d: land_e.at[d - 1]
    )
    value = sums_ref[block(me_e)]
    for d in range(1, count_e):
        value += land_e[d - 1].astype(f32)
    land_r[me_r] = value.astype(bf16)
    mine = land_r.at[me_r]
    exchange("region", count_r, me_r, lambda peer: mine, lambda d: mine)
    value = land_r[0].astype(f32)
    for at in range(1, count_r):
        value += land_r[at].astype(f32)
    full[block(me_e)] = value.astype(bf16)
    own = full.at[block(me_e)]
    exchange("enc", count_e, me_e, lambda peer: own, lambda d: own)
    out_ref[...] = full[...]


def unpack(
    full_ref, stem_ref, gain_ref, shift_ref, kernel_ref, norm_ref, expand_ref, bias_ref, reduce_ref,
    scale_ref,
):
    patch, channels = stem_ref.shape
    hidden = expand_ref.shape[1]
    full = full_ref[...].astype(f32)
    start = first_single(patch)
    stem_ref[...] = full[:patch, :channels]
    kernel_ref[...] = full[patch:start, :channels]
    for at, ref in enumerate((gain_ref, shift_ref, norm_ref, scale_ref)):
        ref[...] = full[start + at : start + at + 1, :channels]
    top = first_bias(patch)
    parts = range(hidden // LANES)
    for at in parts:
        bias_ref[at * LANES : (at + 1) * LANES] = full[top + at]
    top += len(parts)
    for ref in (expand_ref, reduce_ref):
        for at in parts:
            ref[:, at * LANES : (at + 1) * LANES] = full[top : top + channels]
            top += channels


def summed_over_devices(sums, weights):
    (ws, stem_gain, stem_shift, kernel, block_gain, we, bias, wr, layer_scale) = weights
    count_e = lax.axis_size("enc")
    count_r = lax.axis_size("region")
    size = sums.shape[0] // count_e
    copies = 2 * (count_e - 1) + count_r - 1
    vmem = pl.BlockSpec(memory_space=pltpu.VMEM)
    full = pl.pallas_call(
        add_up,
        in_specs=[vmem],
        out_specs=vmem,
        out_shape=jax.ShapeDtypeStruct(sums.shape, bf16),
        scratch_shapes=[
            pltpu.VMEM(sums.shape, bf16),
            pltpu.VMEM((count_e - 1, size, LANES), bf16),
            pltpu.VMEM((count_r, size, LANES), bf16),
            pltpu.VMEM(sums.shape, bf16),
            pltpu.SemaphoreType.DMA((copies,)),
            pltpu.SemaphoreType.DMA((copies,)),
        ],
        compiler_params=pltpu.CompilerParams(collective_id=0, has_side_effects=True),
    )(sums)
    shapes = [
        ws.shape[::-1], (1, stem_gain.shape[0]), (1, stem_shift.shape[0]), kernel.shape[::-1],
        (1, block_gain.shape[0]), we.shape[::-1], bias.shape, wr.shape, (1, layer_scale.shape[0]),
    ]
    outs = pl.pallas_call(
        unpack,
        in_specs=[vmem],
        out_specs=[vmem] * len(shapes),
        out_shape=[jax.ShapeDtypeStruct(shape, f32) for shape in shapes],
    )(full)
    stem, gain, shift, kernel, norm, expand, bias, reduce, scale = outs
    return (
        stem.T, gain[0], shift[0], kernel.T, norm[0], expand.T, bias, reduce, scale[0],
    )


def on_device(pixels, feature_grad, tissue_count, *weights):
    share = 16 * lax.axis_size("enc")
    features, sums = encode_slots(pixels, feature_grad, tissue_count, weights, share)
    return (features, *summed_over_devices(sums, weights))


def solution(mesh):
    return jax.shard_map(
        on_device,
        mesh=mesh,
        in_specs=(
            P(("region", "enc"), None, None),
            P(("region", "enc"), None, None),
            P(("region", "enc")),
        )
        + (P(),) * 9,
        out_specs=(P(("region", "enc"), None, None),) + (P(),) * 9,
        check_vma=False,
    )
```

```python
import jax
import jax.numpy as jnp
import numpy as np
from jax import lax
from jax.experimental import pallas as pl
from jax.experimental.pallas import tpu as pltpu
from jax.sharding import PartitionSpec as P

SIDE = 64
KSIZE = 7
EPS = 1e-06
LANES = 128
CHUNK = 512
PAD = 2
BLOCKS = 8
HALF_PEAK = -0.3257480647361595
EXACT = lax.Precision.HIGHEST
MESH = pl.DeviceIdType.MESH

f32 = jnp.float32
bf16 = jnp.bfloat16


def dot(a, b, dims=((1,), (0,))):
    return lax.dot_general(a, b, (dims, ((), ())), preferred_element_type=f32)


def wide(value, times):
    return jnp.concatenate([value] * times, axis=1)


def fold(value):
    total = value[:, :LANES]
    for at in range(LANES, value.shape[1], LANES):
        total = total + value[:, at : at + LANES]
    return total


def unit(values):
    centre = jnp.mean(values, axis=0, keepdims=True)
    shifted = values - centre
    spread = jnp.mean(jnp.square(shifted), axis=0, keepdims=True)
    scale = lax.rsqrt(spread + EPS)
    return shifted * scale, scale


def gelu_twice(x):
    shape = 1.0 + lax.erf(x * 0.7071067811865476)
    shape = shape.astype(bf16)
    x = x.astype(bf16)
    decay = jnp.exp2(x * x * bf16(-0.7213475204444817) + bf16(HALF_PEAK))
    return x * shape, shape + x * decay


def body(
    count_ref, pix_hbm, grad_hbm, wst_ref, gain_ref, shift_ref, norm_ref, scale_ref, kernel_ref,
    wet_in_ref, bias_ref, wr_ref, place_ref, place_back_ref, pick_ref, feat_hbm, sums_ref, base_s,
    mix_s, pix_v, grad_v, feat_v, par_ref, ws_ref, we_ref, wet_ref, wrt_ref, wrs_ref, taps_ref,
    back_ref, dws_ref, dvec_ref, dwe_ref, dwr_ref, dk_ref, pix_sem, grad_sem, feat_sem,
):
    slots, channels, area = grad_v.shape
    patch = pix_v.shape[1]
    count = count_ref[0]
    pairs = area // LANES
    per = CHUNK // LANES
    chunks = area // CHUNK
    hidden = we_ref.shape[0]
    rows = slots

    def pix_copy(slot):
        return pltpu.make_async_copy(pix_hbm.at[slot], pix_v.at[slot], pix_sem.at[slot])

    def grad_copy(slot):
        return pltpu.make_async_copy(grad_hbm.at[slot], grad_v.at[slot], grad_sem.at[slot])

    def feat_copy(slot, side):
        return pltpu.make_async_copy(feat_v.at[side], feat_hbm.at[slot], feat_sem.at[side])

    @pl.loop(0, count)
    def _(slot):
        pix_copy(slot).start()

    row_at = lax.broadcasted_iota(jnp.int32, (SIDE, LANES), 0)
    lane_at = lax.broadcasted_iota(jnp.int32, (SIDE, LANES), 1) % SIDE
    near = jnp.abs(row_at - lane_at) <= KSIZE // 2
    row_all = lax.broadcasted_iota(jnp.int32, (LANES, LANES), 0)
    lane_all = lax.broadcasted_iota(jnp.int32, (LANES, LANES), 1)
    same = row_all // SIDE == lane_all // SIDE
    mirror = (same & (row_all % SIDE + lane_all % SIDE == SIDE - 1)).astype(f32).astype(bf16)

    def read(ref, slot, chunk):
        return jnp.concatenate(
            [
                ref[PAD + chunk * per + at, pl.ds(slot, channels, stride=rows), :]
                for at in range(per)
            ],
            axis=1,
        )

    def write(ref, slot, chunk, value):
        for at in range(per):
            ref[PAD + chunk * per + at, pl.ds(slot, channels, stride=rows), :] = value[
                :, at * LANES : (at + 1) * LANES
            ]

    def param(at):
        return wide(par_ref[at], per)

    def toeplitz(ref, c):
        blocks = []
        for m in range(BLOCKS):
            row = jnp.broadcast_to(ref[m, pl.ds(c, 1), :], (SIDE, LANES))
            turned = pltpu.roll(row, 0, 1, stride=1, stride_axis=0)
            blocks.append(jnp.where(near, turned, 0.0).astype(bf16))
        return jnp.concatenate(blocks, axis=0)

    lane_rows = lax.broadcasted_iota(jnp.int32, (pairs * rows, LANES), 1)

    def gathered(ref, c):
        at = pl.multiple_of(c * rows, rows)
        full = ref[:, pl.ds(at, rows), :]
        even = full.reshape((pairs + 2 * PAD) * rows, LANES).astype(bf16)
        odd = full[1 : pairs + 3].reshape((pairs + 2) * rows, LANES).astype(bf16)
        size = pairs * rows
        ends = jnp.where(lane_rows < SIDE, even[4 * rows : 4 * rows + size], even[:size])
        return jnp.concatenate(
            [odd[:size], even[2 * rows : 2 * rows + size], odd[2 * rows : 2 * rows + size], ends],
            axis=1,
        )

    edge = jnp.zeros((PAD, channels * rows, LANES), f32)
    for ref in (base_s, mix_s):
        ref[:PAD] = edge
        ref[PAD + pairs :] = edge
    for ref in (dws_ref, dvec_ref, dwe_ref, dwr_ref):
        ref[...] = jnp.zeros(ref.shape, f32)
    for at, ref in enumerate((gain_ref, shift_ref, norm_ref, scale_ref)):
        par_ref[at] = jnp.transpose(jnp.broadcast_to(ref[...], (LANES, channels)))
    kernel = jnp.transpose(kernel_ref[...]).astype(bf16)
    for m in range(BLOCKS):
        taps_ref[m] = dot(kernel, place_ref[m])
        back_ref[m] = dot(kernel, place_back_ref[m])
    stem = jnp.transpose(wst_ref[...].astype(f32))
    stem = stem - jnp.mean(stem, axis=0, keepdims=True)
    high = stem.astype(bf16)
    ws_ref[:, :patch] = high
    ws_ref[:, patch:] = (stem - high.astype(f32)).astype(bf16)
    weight = wet_in_ref[...].astype(f32) * wide(par_ref[2], hidden // LANES)
    weight = weight - jnp.mean(weight, axis=0, keepdims=True)
    wet_ref[...] = weight.astype(bf16)
    weight = jnp.transpose(weight)
    scaled = wr_ref[...].astype(f32) * (0.5 * wide(par_ref[3], hidden // LANES))
    wrs_ref[...] = scaled.astype(bf16)
    wrt_ref[...] = jnp.transpose(scaled).astype(bf16)
    bias = jnp.transpose(jnp.broadcast_to(bias_ref[...][None], (LANES, hidden)))
    high = bias.astype(bf16).astype(f32)
    middle = (bias - high).astype(bf16).astype(f32)
    low = bias - high - middle
    lane = lax.broadcasted_iota(jnp.int32, (hidden, LANES), 1)
    extra = jnp.where(
        lane == channels,
        high,
        jnp.where(lane == channels + 1, middle, jnp.where(lane == channels + 2, low, 0.0)),
    )
    we_ref[...] = extra.astype(bf16)
    we_ref[:, :channels] = weight.astype(bf16)

    def stem_hat(slot, at):
        pix = pix_v[slot, :, pl.ds(at, CHUNK)]
        out = dot(ws_ref[...], jnp.concatenate([pix, pix], axis=0))
        spread = jnp.mean(jnp.square(out), axis=0, keepdims=True)
        scale = lax.rsqrt(spread + EPS)
        return out * scale, scale, pix

    @pl.loop(0, count)
    def _(slot):
        pix_copy(slot).wait()

        grad_copy(slot).start()

        @pl.loop(0, chunks, unroll=8)
        def _(chunk):
            at = pl.multiple_of(chunk * CHUNK, CHUNK)
            hat, _, _ = stem_hat(slot, at)
            write(base_s, slot, chunk, hat * param(0) + param(1))

    @pl.loop(count, slots)
    def _(slot):
        @pl.loop(0, chunks)
        def _(chunk):
            write(base_s, slot, chunk, jnp.zeros((channels, CHUNK), f32))

    @pl.loop(0, channels, unroll=16)
    def _(c):
        out = dot(gathered(base_s, c), toeplitz(taps_ref, c))
        at = pl.multiple_of(c * rows, rows)
        mix_s[PAD : PAD + pairs, pl.ds(at, rows), :] = out.reshape(pairs, rows, LANES)

    @pl.loop(0, count)
    def _(slot):
        side = slot % 2
        grad_copy(slot).wait()

        @pl.when(slot >= 2)
        def _():
            feat_copy(slot, side).wait()

        @pl.loop(0, chunks, unroll=8)
        def _(chunk):
            at = pl.multiple_of(chunk * CHUNK, CHUNK)
            hat, scale = unit(read(mix_s, slot, chunk))
            normed = jnp.concatenate(
                [hat.astype(bf16), jnp.ones((LANES - channels, CHUNK), bf16)], axis=0
            )
            grad = grad_v[slot, :, pl.ds(at, CHUNK)]
            ex = dot(we_ref[...], normed)
            dh = dot(wrt_ref[...], grad).astype(bf16)
            acts, slopes = [], []
            for h in range(0, hidden, 16):
                act, slope = gelu_twice(ex[h : h + 16])
                acts.append(act)
                slopes.append(slope * dh[h : h + 16])
            hid = jnp.concatenate(acts, axis=0)
            de = jnp.concatenate(slopes, axis=0)
            reduced = dot(wrs_ref[...], hid)
            feat_v[side, :, pl.ds(at, CHUNK)] = (read(base_s, slot, chunk) + reduced).astype(bf16)
            dwr_ref[:, :channels] += dot(hid, grad, ((1,), (1,)))
            dwe_ref[...] += dot(de, normed, ((1,), (1,)))
            dn = dot(wet_ref[...], de)
            second = jnp.mean(dn * hat, axis=0, keepdims=True)
            write(mix_s, slot, chunk, scale * (dn - hat * second))

        feat_copy(slot, side).start()

    @pl.loop(count, slots)
    def _(slot):
        side = slot % 2

        @pl.when(slot >= 2)
        def _():
            feat_copy(slot, side).wait()

        @pl.loop(0, chunks)
        def _(chunk):
            at = pl.multiple_of(chunk * CHUNK, CHUNK)
            feat_v[side, :, pl.ds(at, CHUNK)] = jnp.zeros((channels, CHUNK), bf16)

        feat_copy(slot, side).start()

    lane_one = lax.broadcasted_iota(jnp.int32, (8, LANES), 1)
    lane_half = lane_one % SIDE
    lower = (lane_one >= 3) & (lane_one < SIDE + 3)

    def banded(cross, r, k, turn):
        def tall(v):
            return cross[r * SIDE + 8 * v : r * SIDE + 8 * v + 8, k * LANES : (k + 1) * LANES]

        even = jnp.where(lane_half < 4, 0.0, tall(6))
        for v in (4, 2, 0):
            even = jnp.where(lane_half >= 52 - 8 * v, tall(v), even)
        odd = tall(7)
        for v in (5, 3, 1):
            odd = jnp.where(lane_half >= 52 - 8 * v, tall(v), odd)
        odd = jnp.where(lane_half >= 60, 0.0, odd)
        return pltpu.roll(even, turn, 1, stride=1, stride_axis=0) + pltpu.roll(
            odd, turn + 8, 1, stride=1, stride_axis=0
        )

    @pl.loop(0, channels, unroll=8)
    def _(c):
        at = pl.multiple_of(c * rows, rows)
        grad = mix_s[PAD : PAD + pairs, pl.ds(at, rows), :]
        grad = grad.reshape(pairs * rows, LANES).astype(bf16)
        grad = dot(mirror, grad, ((1,), (1,))).astype(bf16)
        cross = dot(grad, gathered(base_s, c))
        first = [banded(cross, 0, k, 0) for k in (3, 0, 1, 2)]
        second = [banded(cross, 1, k, SIDE) for k in (0, 1, 2, 3)]
        taken = [second[0]] + [
            jnp.where(lower, second[k - 1], second[k]) for k in range(1, 4)
        ]
        for k in range(4):
            dk_ref[k, pl.ds(c, 1), :] = jnp.sum(first[k] + taken[k], axis=0, keepdims=True)
        out = dot(gathered(mix_s, c), toeplitz(back_ref, c))
        mix_s[PAD : PAD + pairs, pl.ds(at, rows), :] = out.reshape(pairs, rows, LANES)

    @pl.loop(0, count)
    def _(slot):
        @pl.loop(0, chunks, unroll=4)
        def _(chunk):
            at = pl.multiple_of(chunk * CHUNK, CHUNK)
            hat, scale, pix = stem_hat(slot, at)
            dbase = grad_v[slot, :, pl.ds(at, CHUNK)].astype(f32) + read(mix_s, slot, chunk)
            dvec_ref[...] += fold(dbase)
            second = jnp.mean(dbase * hat * param(0), axis=0, keepdims=True)
            straight = (scale * dbase).astype(bf16)
            along = (hat * (scale * second)).astype(bf16)
            both = dot(jnp.concatenate([straight, along], axis=0), pix, ((1,), (1,)))
            dws_ref[:, :, :patch] += both.reshape(2, channels, patch)

    mixed = dws_ref[0] * par_ref[0] - dws_ref[1]
    mixed = mixed - jnp.mean(mixed, axis=0, keepdims=True)
    for at in range(4):
        mixed += lax.dot_general(
            dk_ref[at], pick_ref[at], (((1,), (0,)), ((), ())), precision=EXACT,
            preferred_element_type=f32,
        )
    products = jnp.transpose(dwr_ref[...])[:channels] * 0.5
    expand = jnp.transpose(dwe_ref[...])
    stem = ws_ref[:, :patch].astype(f32) + ws_ref[:, patch:].astype(f32)
    singles = [
        jnp.sum(dws_ref[0, :, :patch] * stem, axis=1, keepdims=True),
        jnp.sum(dvec_ref[...], axis=1, keepdims=True),
    ]
    singles.append(
        jnp.sum(expand[:channels] * wet_in_ref[...].astype(f32), axis=1, keepdims=True)
    )
    singles.append(jnp.sum(products * wr_ref[...].astype(f32), axis=1, keepdims=True))
    lane = lax.broadcasted_iota(jnp.int32, (channels, LANES), 1)
    start = first_single(patch)
    for at, single in enumerate(singles):
        mixed = jnp.where(lane == start + at, single, mixed)
    mixed = jnp.concatenate([mixed, jnp.zeros((LANES - channels, LANES), f32)], axis=0)
    top = first_bias(patch)
    sums_ref[:top] = jnp.transpose(mixed)[:top]
    products = products * wide(par_ref[3], hidden // LANES)
    tail = expand[channels : channels + 1]
    expand = expand[:channels] * wide(par_ref[2], hidden // LANES)
    for at in range(hidden // LANES):
        sums_ref[top : top + 1] = tail[:, at * LANES : (at + 1) * LANES]
        top += 1
    for value in (expand, products):
        for at in range(hidden // LANES):
            sums_ref[top : top + channels] = value[:, at * LANES : (at + 1) * LANES]
            top += channels
    if top < sums_ref.shape[0]:
        sums_ref[top:] = jnp.zeros((sums_ref.shape[0] - top, LANES), f32)
    for side in range(min(2, slots)):
        feat_copy(side, side).wait()


def first_single(patch):
    return patch + KSIZE * KSIZE


def first_bias(patch):
    return first_single(patch) + 4


def total_rows(patch, channels, hidden, share):
    blocks = hidden // LANES
    total = first_bias(patch) + blocks + 2 * channels * blocks
    return -(-total // share) * share


def tap_places(patch):
    half = KSIZE // 2
    taps = KSIZE * KSIZE
    place = np.zeros((BLOCKS, taps, LANES), np.float32)
    for at, m in enumerate((2, 3, 4, 5, 6, 7, 8, 1)):
        for r in range(2):
            a = m - 2 * PAD - r
            if abs(a) > half:
                continue
            for b in range(-half, half + 1):
                place[at, (a + half) * KSIZE + b + half, (r * SIDE - b) % LANES] = 1.0
    pick = np.zeros((4, LANES, LANES), np.float32)
    for k in range(4):
        for rr in range(2):
            a = 2 * (k - PAD) + rr
            if abs(a) > half:
                continue
            for b in range(-half, half + 1):
                for step in range(4):
                    lane = (rr * SIDE + SIDE - 1 - 16 * step + b) % LANES
                    pick[k, lane, patch + (a + half) * KSIZE + b + half] = 1.0
    return place, pick


def encode_slots(pixels, feature_grad, count, weights, share=1):
    (ws, stem_gain, stem_shift, kernel, block_gain, we, bias, wr, layer_scale) = weights
    slots, patch, area = pixels.shape
    channels = ws.shape[0]
    hidden = we.shape[0]
    pairs = area // LANES
    place, pick = tap_places(patch)
    total = total_rows(patch, channels, hidden, share)
    consts = (
        ws.T, stem_gain[None], stem_shift[None], block_gain[None], layer_scale[None], kernel.T,
        we.T, bias, wr, jnp.asarray(place, bf16),
        jnp.asarray(place[:, ::-1], bf16), jnp.asarray(pick),
    )
    vmem = pl.BlockSpec(memory_space=pltpu.VMEM)
    hbm = pl.BlockSpec(memory_space=pl.ANY)
    return pl.pallas_call(
        body,
        in_specs=[pl.BlockSpec(memory_space=pltpu.SMEM), hbm, hbm] + [vmem] * len(consts),
        out_specs=[hbm, vmem],
        scratch_shapes=[
            pltpu.VMEM((pairs + 2 * PAD, channels * slots, LANES), f32),
            pltpu.VMEM((pairs + 2 * PAD, channels * slots, LANES), f32),
            pltpu.VMEM((slots, patch, area), bf16),
            pltpu.VMEM((slots, channels, area), bf16),
            pltpu.VMEM((2, channels, area), bf16),
            pltpu.VMEM((4, channels, LANES), f32),
            pltpu.VMEM((channels, 2 * patch), bf16),
            pltpu.VMEM((hidden, LANES), bf16),
            pltpu.VMEM((channels, hidden), bf16),
            pltpu.VMEM((hidden, channels), bf16),
            pltpu.VMEM((channels, hidden), bf16),
            pltpu.VMEM((BLOCKS, channels, LANES), f32),
            pltpu.VMEM((BLOCKS, channels, LANES), f32),
            pltpu.VMEM((2, channels, LANES), f32),
            pltpu.VMEM((channels, LANES), f32),
            pltpu.VMEM((hidden, LANES), f32),
            pltpu.VMEM((hidden, LANES), f32),
            pltpu.VMEM((4, channels, LANES), f32),
            pltpu.SemaphoreType.DMA((slots,)),
            pltpu.SemaphoreType.DMA((slots,)),
            pltpu.SemaphoreType.DMA((2,)),
        ],
        out_shape=[
            jax.ShapeDtypeStruct((slots, channels, area), bf16),
            jax.ShapeDtypeStruct((total, LANES), f32),
        ],
        compiler_params=pltpu.CompilerParams(vmem_limit_bytes=60 * 2**20),
    )(count, pixels, feature_grad, *consts)


def add_up(sums_ref, out_ref, outgoing, land_e, land_r, full, out_sems, in_sems):
    count_e = lax.axis_size("enc")
    count_r = lax.axis_size("region")
    me_e = lax.axis_index("enc")
    me_r = lax.axis_index("region")
    barrier = pltpu.get_barrier_semaphore()
    for d in range(1, count_e):
        pl.semaphore_signal(
            barrier, 1, device_id={"enc": lax.rem(me_e + d, count_e)}, device_id_type=MESH
        )
    for d in range(1, count_r):
        pl.semaphore_signal(
            barrier, 1, device_id={"region": lax.rem(me_r + d, count_r)}, device_id_type=MESH
        )
    outgoing[...] = sums_ref[...].astype(bf16)
    pl.semaphore_wait(barrier, count_e + count_r - 2)
    size = land_e.shape[1]
    sems = iter(range(2 * (count_e - 1) + count_r - 1))

    def block(index):
        return pl.ds(pl.multiple_of(index * size, 16), size)

    def exchange(axis, count, me, source, target):
        copies = []
        for d in range(1, count):
            peer = lax.rem(me + d, count)
            sem = next(sems)
            copy = pltpu.make_async_remote_copy(
                src_ref=source(peer), dst_ref=target(d), send_sem=out_sems.at[sem],
                recv_sem=in_sems.at[sem], device_id={axis: peer}, device_id_type=MESH,
            )
            copy.start()
            copies.append(copy)
        for copy in copies:
            copy.wait()

    exchange(
        "enc", count_e, me_e, lambda peer: outgoing.at[block(peer)], lambda d: land_e.at[d - 1]
    )
    value = sums_ref[block(me_e)]
    for d in range(1, count_e):
        value += land_e[d - 1].astype(f32)
    land_r[me_r] = value.astype(bf16)
    mine = land_r.at[me_r]
    exchange("region", count_r, me_r, lambda peer: mine, lambda d: mine)
    value = land_r[0].astype(f32)
    for at in range(1, count_r):
        value += land_r[at].astype(f32)
    full[block(me_e)] = value.astype(bf16)
    own = full.at[block(me_e)]
    exchange("enc", count_e, me_e, lambda peer: own, lambda d: own)
    out_ref[...] = full[...]


def unpack(
    full_ref, stem_ref, gain_ref, shift_ref, kernel_ref, norm_ref, expand_ref, bias_ref, reduce_ref,
    scale_ref,
):
    patch, channels = stem_ref.shape
    hidden = expand_ref.shape[1]
    full = full_ref[...].astype(f32)
    start = first_single(patch)
    stem_ref[...] = full[:patch, :channels]
    kernel_ref[...] = full[patch:start, :channels]
    for at, ref in enumerate((gain_ref, shift_ref, norm_ref, scale_ref)):
        ref[...] = full[start + at : start + at + 1, :channels]
    top = first_bias(patch)
    parts = range(hidden // LANES)
    for at in parts:
        bias_ref[at * LANES : (at + 1) * LANES] = full[top + at]
    top += len(parts)
    for ref in (expand_ref, reduce_ref):
        for at in parts:
            ref[:, at * LANES : (at + 1) * LANES] = full[top : top + channels]
            top += channels


def summed_over_devices(sums, weights):
    (ws, stem_gain, stem_shift, kernel, block_gain, we, bias, wr, layer_scale) = weights
    count_e = lax.axis_size("enc")
    count_r = lax.axis_size("region")
    size = sums.shape[0] // count_e
    copies = 2 * (count_e - 1) + count_r - 1
    vmem = pl.BlockSpec(memory_space=pltpu.VMEM)
    full = pl.pallas_call(
        add_up,
        in_specs=[vmem],
        out_specs=vmem,
        out_shape=jax.ShapeDtypeStruct(sums.shape, bf16),
        scratch_shapes=[
            pltpu.VMEM(sums.shape, bf16),
            pltpu.VMEM((count_e - 1, size, LANES), bf16),
            pltpu.VMEM((count_r, size, LANES), bf16),
            pltpu.VMEM(sums.shape, bf16),
            pltpu.SemaphoreType.DMA((copies,)),
            pltpu.SemaphoreType.DMA((copies,)),
        ],
        compiler_params=pltpu.CompilerParams(collective_id=0, has_side_effects=True),
    )(sums)
    shapes = [
        ws.shape[::-1], (1, stem_gain.shape[0]), (1, stem_shift.shape[0]), kernel.shape[::-1],
        (1, block_gain.shape[0]), we.shape[::-1], bias.shape, wr.shape, (1, layer_scale.shape[0]),
    ]
    outs = pl.pallas_call(
        unpack,
        in_specs=[vmem],
        out_specs=[vmem] * len(shapes),
        out_shape=[jax.ShapeDtypeStruct(shape, f32) for shape in shapes],
    )(full)
    stem, gain, shift, kernel, norm, expand, bias, reduce, scale = outs
    return (
        stem.T, gain[0], shift[0], kernel.T, norm[0], expand.T, bias, reduce, scale[0],
    )


def on_device(pixels, feature_grad, tissue_count, *weights):
    share = 16 * lax.axis_size("enc")
    features, sums = encode_slots(pixels, feature_grad, tissue_count, weights, share)
    return (features, *summed_over_devices(sums, weights))


def solution(mesh):
    return jax.shard_map(
        on_device,
        mesh=mesh,
        in_specs=(
            P(("region", "enc"), None, None),
            P(("region", "enc"), None, None),
            P(("region", "enc")),
        )
        + (P(),) * 9,
        out_specs=(P(("region", "enc"), None, None),) + (P(),) * 9,
        check_vma=False,
    )
```
